768 devices in a mesh: row: 96 (over x, z, core), col: 8 (over y).
Axes of the slice: x: 4, y: 8, z: 12, core: 2. Of those that a mesh axis runs over, the one named last changes fastest.
Arguments:
- obs_resid: float32 [96, 32768], P('row', 'col'), may hold values from -6 to 6
- obs_cell: int32 [96, 32768], P('row', 'col'), may hold values from 0 to 66559
- azimuth: float32 [96, 32768], P('row', 'col'), may hold values from -3.140625 to 3.140625
- gate_count: int32 [96, 8], P('row', 'col'), may hold values from 1024 to 4096, as said below
- kappa_xx: float32 [65, 768, 1024], P(None, 'row', 'col'), may hold values from 0.1 to 0.2
- kappa_yy: float32 [65, 768, 1024], P(None, 'row', 'col'), may hold values from 0.1 to 0.2
- kappa_shear: float32 [65, 768, 1024], P(None, 'row', 'col'), may hold values from -0.24 to 0.24
- norm_scale: float32 [2, 65, 768, 1024], P(None, None, 'row', 'col'), may hold values from 0.5 to 2
Outputs:
- control_grad: float32 [2, 65, 768, 1024], P(None, None, 'row', 'col')
The draws below stay inside these ranges and needn't reach their ends.
Inputs may be any that keep to these rules, and one draw needn't show every extreme that they name: `gate_count`: some tile has all 4096 slots live.
All inputs are finite; a program needn't handle non-finite values.
Results may differ from the reference program's by a relative error of at most 0.00002.
Values sent between devices are 32-bit elements; how exact they have to be, the bound alone decides.
No kernel may reach another device: no remote copies, remote signals or barrier semaphores. Data moves between devices by JAX's collectives and lax.ppermute only.
A program may use at most 32 MiB of HBM per device.

```python
import math
import jax
import jax.numpy as jnp

L = 65
CY = 8
CX = 128
OBS_DEV = 4096
STEPS = 4
NY = 768
NX = 1024
N_ROW = 96
N_COL = 8


def draw_gate_count(key, part):
    first, second = jax.random.split(jax.random.fold_in(key, 7))
    counts = jax.random.randint(first, (N_ROW * N_COL,), OBS_DEV // 4, OBS_DEV + 1)
    chosen = jax.random.randint(second, (), 0, N_ROW * N_COL)
    flat = jnp.where(jnp.arange(N_ROW * N_COL) == chosen, OBS_DEV, counts)
    return flat.reshape(N_ROW, N_COL).astype(jnp.int32)


def touch_ends(entries, stream_key, smallest, largest):
    longest = entries.shape.index(max(entries.shape))
    spots = []
    for shift in (0, 1):
        where = [jax.random.randint(jax.random.fold_in(stream_key, axis), (), 0, length) for axis, length in enumerate(entries.shape)]
        where[longest] = (where[longest] + shift) % entries.shape[longest]
        spots.append(tuple(where))
    return entries.at[spots[0]].set(smallest).at[spots[1]].set(largest)


def block_scale(rng, extent, shards, least, largest):
    def one(position, parts):
        steps = jax.random.uniform(jax.random.fold_in(jax.random.fold_in(rng, 6), position), (parts,), jnp.float32, least / len(shards), largest / len(shards))
        return jnp.repeat(jnp.exp(steps), extent[position] // parts).reshape((-1,) + (1,) * (len(extent) - position - 1))

    loudness = one(*shards[0])
    for cut in shards[1:]:
        loudness = loudness * one(*cut)
    return loudness


def centred(rng, shape, scale, bound, pieces=(), kind=jnp.bfloat16):
    result = scale * jax.random.normal(rng, shape, jnp.float32)
    if pieces:
        result = result * block_scale(rng, shape, pieces, -0.22, 0.18)
    return jnp.clip(result, -bound, bound).astype(kind)


def setup_inputs(seed: int = 0) -> dict:
    arg_keys = jax.random.split(jax.random.key(seed), 9)
    return {
        "obs_resid": centred(arg_keys[0], (N_ROW, N_COL * OBS_DEV), 1.0, 6.0, ((0, 96), (1, 8)), jnp.float32),
        "obs_cell": touch_ends(jax.random.randint(arg_keys[1], (N_ROW, N_COL * OBS_DEV), 0, L * CY * CX), jax.random.fold_in(arg_keys[1], 1), 0, (L * CY * CX) - 1).astype(jnp.int32),
        "azimuth": jnp.clip(jax.random.uniform(arg_keys[2], (N_ROW, N_COL * OBS_DEV), jnp.float32, -3.140625, 3.140625), -3.140625, 3.140625),
        "gate_count": draw_gate_count(jax.random.fold_in(arg_keys[8], 71), 0),
        "kappa_xx": jnp.clip(jnp.exp(math.log(0.2) - 0.6931472 * jax.random.uniform(arg_keys[4], (L, NY, NX), jnp.float32) ** block_scale(arg_keys[4], (L, NY, NX), ((1, 96), (2, 8)), -0.2, 0.2)), 0.1, 0.2),
        "kappa_yy": jnp.clip(jnp.exp(math.log(0.2) - 0.6931472 * jax.random.uniform(arg_keys[5], (L, NY, NX), jnp.float32) ** block_scale(arg_keys[5], (L, NY, NX), ((1, 96), (2, 8)), -0.2, 0.2)), 0.1, 0.2),
        "kappa_shear": jnp.clip(jax.random.uniform(arg_keys[6], (L, NY, NX), jnp.float32, -0.24, 0.24) * block_scale(arg_keys[6], (L, NY, NX), ((1, 96), (2, 8)), -0.4, 0.0), -0.24, 0.24),
        "norm_scale": jnp.clip(jnp.exp(math.log(2.0) - 1.3862944 * jax.random.uniform(arg_keys[7], (2, L, NY, NX), jnp.float32) ** block_scale(arg_keys[7], (2, L, NY, NX), ((2, 96), (3, 8)), -0.2, 0.2)), 0.5, 2.0),
    }


def relax(field, kappa):
    coef_xx = kappa[0, :, :-1, :-1]
    coef_xy = kappa[1, :, :-1, :-1]
    coef_yy = kappa[2, :, :-1, :-1]
    grad_x = field[..., :-1, 1:] - field[..., :-1, :-1]
    grad_y = field[..., 1:, :-1] - field[..., :-1, :-1]
    flux_x = coef_xx * grad_x + coef_xy * grad_y
    flux_y = coef_xy * grad_x + coef_yy * grad_y
    spread = flux_x[..., 1:, :-1] - flux_x[..., 1:, 1:] + flux_y[..., :-1, 1:] - flux_y[..., 1:, 1:]
    return field[..., 1:-1, 1:-1] - spread

def pad_plane(array):
    widths = [(0, 0)] * (array.ndim - 2) + [(1, 1), (1, 1)]
    return jnp.pad(array, widths)

def reference(obs_resid, obs_cell, azimuth, gate_count, kappa_xx, kappa_yy, kappa_shear, norm_scale):
    total_y = CY * N_ROW
    total_x = CX * N_COL
    resid = obs_resid.reshape(N_ROW, N_COL, OBS_DEV)
    cells = obs_cell.reshape(N_ROW, N_COL, OBS_DEV)
    angles = azimuth.reshape(N_ROW, N_COL, OBS_DEV)
    slots = jnp.arange(OBS_DEV, dtype=jnp.int32)[None, None, :]
    weight = jnp.where(slots < gate_count[:, :, None], resid, jnp.zeros_like(resid))
    level = cells // (CY * CX)
    remain = cells % (CY * CX)
    tile_r = jnp.arange(N_ROW, dtype=jnp.int32)[:, None, None]
    tile_c = jnp.arange(N_COL, dtype=jnp.int32)[None, :, None]
    glob_y = tile_r * CY + remain // CX
    glob_x = tile_c * CX + remain % CX
    target = ((level * total_y + glob_y) * total_x + glob_x).astype(jnp.int32).reshape(-1)
    count = L * total_y * total_x
    wind_u = jax.ops.segment_sum((weight * jnp.sin(angles)).reshape(-1), target, num_segments=count)
    wind_v = jax.ops.segment_sum((weight * jnp.cos(angles)).reshape(-1), target, num_segments=count)
    wind = jnp.stack([wind_u, wind_v]).reshape(2, L, total_y, total_x)
    padded = pad_plane(wind)
    along_y = 0.5 * (padded[..., 2:, 1:-1] - padded[..., :-2, 1:-1])
    along_x = 0.5 * (padded[..., 1:-1, 2:] - padded[..., 1:-1, :-2])
    stream = along_y[0] - along_x[1]
    potential = -along_x[0] - along_y[1]
    field = jnp.stack([stream, potential])
    kxy = kappa_shear * jnp.sqrt(kappa_xx * kappa_yy)
    kappa = pad_plane(jnp.stack([kappa_xx, kxy, kappa_yy]))
    for index in range(STEPS):
        field = relax(pad_plane(field), kappa)
    return norm_scale * field
```

```python
import jax
import jax.numpy as jnp
from jax import lax
from jax.experimental import pallas as pl
from jax.experimental.pallas import tpu as pltpu
from jax.sharding import PartitionSpec as P

STEPS = 4
NT = 9
LV = 8 * NT
F32 = jnp.float32
BF16 = jnp.bfloat16
KC = 1024
SPLITS = 2
NQ = 81
NM = NQ // 3
VM = pl.BlockSpec(memory_space=pltpu.VMEM)
SM = pl.BlockSpec(memory_space=pltpu.SMEM)


def pairs(size, first):
    out = []
    for i in range(first, size - 1, 2):
        out += [(i, i + 1), (i + 1, i)]
    return out


def roll(x, by):
    by = by % 128
    return x if by == 0 else pltpu.roll(x, by, 1)


def at(ref, i):
    return ref[pl.ds(pl.multiple_of(i * 8, 8), 8), :]


def strided(ref, base, tile, y):
    if tile < 8:
        return ref[pl.ds(base + tile * 64 + y, 8, stride=8), :]
    row = base + 512 + y
    return jnp.broadcast_to(ref[row : row + 1, :], (8, 128))


def lanes():
    return lax.broadcasted_iota(jnp.int32, (8, 128), 1)


def sublanes():
    return lax.broadcasted_iota(jnp.int32, (8, 128), 0)


def prepare(pos, gate, resid, cell, azimuth, kxx, kyy, ksh, pay_a, pay_b, kt):
    odd = (pos[0] & 1) == 1
    slot = lax.broadcasted_iota(jnp.int32, (32, 128), 0) * 128 + lax.broadcasted_iota(
        jnp.int32, (32, 128), 1
    )
    weight = jnp.where(slot < gate[0, 0], resid[...], 0.0)
    angle = azimuth[...]
    wu = weight * jnp.sin(angle)
    wv = weight * jnp.cos(angle)
    cf = cell[...].astype(F32)
    for pay in (pay_a, pay_b):
        pay[0:32, :] = wu
        pay[32:64, :] = wv
        pay[64:96, :] = cf
    for tile in range(NT):
        rows = []
        for y in range(8):
            xx = strided(kxx, 0, tile, y)
            yy = strided(kyy, 0, tile, y)
            xy = strided(ksh, 0, tile, y) * jnp.sqrt(xx * yy)
            rows.append((xx, xy, yy))
            for q in range(3):
                start = (q * 8 + y) * LV + tile * 8
                kt[start : start + 8, :] = rows[y][q]
        for i in range(4):
            for q in range(3):
                start = 96 + (i * 3 + q) * LV + tile * 8
                low, high = rows[i][q], rows[i + 4][q]
                pay_a[start : start + 8, :] = jnp.where(odd, low, high)
                pay_b[start : start + 8, :] = jnp.where(odd, high, low)


def scatter(wu, wv, cf, shift, count, hot, val, tab, out_u, out_v, base):
    cell = cf.astype(jnp.int32)
    level = lax.shift_right_logical(cell, 10)
    y = lax.shift_right_logical(cell, 7) & 7
    tab[0:32, :] = ((y - shift) * LV + level).astype(F32)
    tab[32:64, :] = (cell & 127).astype(F32)
    for n, value in enumerate((wu, wv)):
        for s in range(SPLITS):
            top = value.astype(BF16).astype(F32)
            value = value - top
            start = 64 + (n * SPLITS + s) * 32
            tab[start : start + 32, :] = top
    rows = lax.broadcasted_iota(jnp.int32, (count, 128), 0).astype(F32)
    cols = lax.broadcasted_iota(jnp.int32, (128, 128), 0).astype(F32)
    per = KC // 128

    def chunk(c, _):
        for j in range(per):
            i = c * per + j
            span = slice(j * 128, j * 128 + 128)
            row = tab[pl.ds(i, 1), :]
            hot[0:count, span] = jnp.where(rows == row, 1.0, 0.0).astype(BF16)
            col = tab[pl.ds(32 + i, 1), :]
            hit = cols == col
            for s in range(SPLITS):
                for n in range(2):
                    part = tab[pl.ds(64 + (n * SPLITS + s) * 32 + i, 1), :]
                    val[s * 256 + n * 128 : s * 256 + n * 128 + 128, span] = jnp.where(
                        hit, part, 0.0
                    ).astype(BF16)
        total = None
        for s in range(SPLITS):
            part = lax.dot_general(
                hot[0:count, :],
                val[s * 256 : s * 256 + 256, :],
                (((1,), (1,)), ((), ())),
                preferred_element_type=F32,
            )
            total = part if total is None else total + part

        @pl.when(c == 0)
        def _():
            out_u[base : base + count, :] = total[:, 0:128]
            out_v[base : base + count, :] = total[:, 128:256]

        @pl.when(c > 0)
        def _():
            out_u[base : base + count, :] += total[:, 0:128]
            out_v[base : base + count, :] += total[:, 128:256]

        return 0

    lax.fori_loop(0, 4096 // KC, chunk, 0)


def own_wind(obs, out_u, out_v, hot, val, tab):
    scatter(
        obs[0:32, :], obs[32:64, :], obs[64:96, :], 0, 8 * LV, hot, val, tab, out_u, out_v, 0
    )


def wind_at(own, halo, row, tile):
    if 0 <= row < 8:
        return at(own, row * NT + tile)
    return at(halo, ((row + 5) if row < 0 else row - 3) * NT + tile)


def kappa_at(kt, halo, q, row, tile):
    if 0 <= row < 8:
        return at(kt, (q * 8 + row) * NT + tile)
    return at(halo, (((row + 4) if row < 0 else row - 4) * 3 + q) * NT + tile)


def edges(pos, rec_a, rec_b, u, v, kt, hu, hv, kh, sw, sk, msg_c, msg_d, hot, val, tab):
    odd = (pos[0] & 1) == 1
    north = jnp.where(odd, rec_a[0:96, :], rec_b[0:96, :])
    south = jnp.where(odd, rec_b[0:96, :], rec_a[0:96, :])
    for part, shift, base in ((north, 3, 0), (south, 0, 5 * LV)):
        scatter(
            part[0:32], part[32:64], part[64:96], shift, 5 * LV, hot, val, tab, hu, hv, base
        )
    size = 4 * 3 * LV
    kh[0:size, :] = jnp.where(odd, rec_a[96 : 96 + size, :], rec_b[96 : 96 + size, :])
    rest = 3 * 3 * LV
    kh[size : size + rest, :] = jnp.where(
        odd, rec_b[96 : 96 + rest, :], rec_a[96 : 96 + rest, :]
    )
    lane = lanes()
    left_slot = lane // 16
    right_slot = ((lane + 4) % 128) // 16
    strips = []
    for n, (own, halo) in enumerate(((u, hu), (v, hv))):
        for row in range(-5, 13):
            strips.append((sw, n * 18 + row + 5, lambda t, o=own, h=halo, r=row: wind_at(o, h, r, t)))
    for q in range(3):
        for row in range(-4, 11):
            strips.append((sk, q * 15 + row + 4, lambda t, q=q, r=row: kappa_at(kt, kh, q, r, t)))
    odd_col = (pos[1] & 1) == 1
    fifth = lane % 16
    packed = {}
    for k, (ref, index, get) in enumerate(strips):
        left = right = None
        for j in range(8):
            moved = roll(get(j), 16 * j + 6)
            left = moved if j == 0 else jnp.where(left_slot == j, moved, left)
            right = moved if j == 0 else jnp.where(right_slot == j, moved, right)
        last = roll(get(8), 6)[0:1, :]
        start = index * 24
        ref[start : start + 8, :] = left
        ref[start + 8 : start + 16, :] = right
        ref[start + 16 : start + 24, :] = jnp.broadcast_to(last, (8, 128))
        row = NM * 8 + k
        msg_c[row : row + 1, :] = last
        msg_d[row : row + 1, :] = last
        t = k % 3
        packed[t] = (roll(left, 5 * t), roll(left, 5 * t - 5))
        if t == 2:
            right_edge, left_edge = (
                jnp.where(fifth < 6, packed[0][e], jnp.where(fifth < 11, packed[1][e], packed[2][e]))
                for e in range(2)
            )
            start = (k // 3) * 8
            msg_c[start : start + 8, :] = jnp.where(odd_col, left_edge, right_edge)
            msg_d[start : start + 8, :] = jnp.where(odd_col, right_edge, left_edge)
    fill = NM * 8 + NQ
    for msg in (msg_c, msg_d):
        msg[fill : fill + 7, :] = jnp.zeros((7, 128), F32)


def diffuse(wind, kappa, low, high, mask):
    field = {}
    for row in range(-4, 12):
        side = low if row < 0 else high if row > 7 else None
        across = []
        along = []
        for n in range(2):
            here = wind(n, row)
            across.append(roll(here, -1) - roll(here, 1))
            along.append(wind(n, row + 1) - wind(n, row - 1))
        scale = jnp.full((8, 128), 0.5, F32)
        if side is not None:
            scale = scale * side
        if mask is not None:
            scale = scale * mask
        field[0, row] = scale * (along[0] - across[1])
        field[1, row] = -scale * (across[0] + along[1])
    for step in range(STEPS):
        more = STEPS - 1 - step
        new = {}
        before = {}
        for row in range(-more - 1, 8 + more):
            xx, xy, yy = (kappa(q, row) for q in range(3))
            for n in range(2):
                here = field[n, row]
                gx = roll(here, -1) - here
                gy = field[n, row + 1] - here
                hx = xx * gx + xy * gy
                hy = xy * gx + yy * gy
                if row >= -more:
                    value = here - (roll(hx, 1) - hx + (before[n] - hy))
                    if row > 7:
                        value = value * high
                    if mask is not None:
                        value = value * mask
                    new[n, row] = value
                before[n] = hy
        field = new
    return field


def ends(pos, size):
    low = jnp.where(pos[0] == 0, 0.0, 1.0).astype(F32)
    high = jnp.where(pos[0] == size - 1, 0.0, 1.0).astype(F32)
    return low, high


def middle(size, pos, u, v, hu, hv, kt, kh, main):
    low, high = ends(pos, size)
    wind_refs = ((u, hu), (v, hv))

    def body(tile, _):
        field = diffuse(
            lambda n, row: wind_at(*wind_refs[n], row, tile),
            lambda q, row: kappa_at(kt, kh, q, row, tile),
            low,
            high,
            None,
        )
        for n in range(2):
            for y in range(8):
                start = pl.multiple_of(((n * 8 + y) * NT + tile) * 8, 8)
                main[pl.ds(start, 8), :] = field[n, y]
        return 0

    lax.fori_loop(0, NT, body, 0)


def finish(
    rows, columns, pos, rec_c, rec_d, sw, sk, main, norm, out, mw, mk, masks, sf
):
    low, high = ends(pos, rows)
    odd_col = (pos[1] & 1) == 1
    lane = lanes()
    fifth = lane % 16
    first = sublanes() == 0
    take_left = (fifth >= 1) & (fifth <= 5)
    take_right = (fifth >= 6) & (fifth <= 10)
    for k in range(NQ):
        i, t = k // 3, k % 3
        a = rec_c[i * 8 : i * 8 + 8, :]
        b = rec_d[i * 8 : i * 8 + 8, :]
        from_left = roll(jnp.where(odd_col, a, b), -5 * t)
        from_right = roll(jnp.where(odd_col, b, a), 5 - 5 * t)
        row = NM * 8 + k
        a = jnp.broadcast_to(rec_c[row : row + 1, :], (8, 128))
        b = jnp.broadcast_to(rec_d[row : row + 1, :], (8, 128))
        last = jnp.where(first == odd_col, a, b)
        src, dst, index = (sw, mw, k) if k < 36 else (sk, mk, k - 36)
        start = index * 24
        dst[start : start + 8, :] = jnp.where(take_left, from_left, src[start : start + 8, :])
        dst[start + 8 : start + 16, :] = jnp.where(
            take_right, from_right, src[start + 8 : start + 16, :]
        )
        take = (take_left & first) | (take_right & jnp.logical_not(first))
        dst[start + 16 : start + 24, :] = jnp.where(take, last, src[start + 16 : start + 24, :])
    west = jnp.where(pos[1] == 0, 0.0, 1.0).astype(F32)
    east = jnp.where(pos[1] == columns - 1, 0.0, 1.0).astype(F32)
    left_mask = jnp.where(fifth < 6, west, 1.0)
    right_mask = jnp.where((fifth >= 6) & (fifth < 12), east, 1.0)
    masks[0:8, :] = left_mask
    masks[8:16, :] = right_mask
    masks[16:24, :] = jnp.where(first, left_mask, right_mask)

    def body(tile, _):
        field = diffuse(
            lambda n, row: at(mw, (n * 18 + row + 5) * 3 + tile),
            lambda q, row: at(mk, (q * 15 + row + 4) * 3 + tile),
            low,
            high,
            at(masks, tile),
        )
        for n in range(2):
            for y in range(8):
                start = pl.multiple_of(((n * 8 + y) * 3 + tile) * 8, 8)
                sf[pl.ds(start, 8), :] = field[n, y]
        return 0

    lax.fori_loop(0, 3, body, 0)
    edge = (lane < 5) | (lane >= 123)
    for n in range(2):
        for y in range(8):
            start = (n * 8 + y) * 24
            both = jnp.where(take_left, sf[start + 8 : start + 16, :], sf[start : start + 8, :])
            for tile in range(8):
                place = ((n * 8 + y) * NT + tile) * 8
                value = jnp.where(edge, roll(both, -(16 * tile + 6)), main[place : place + 8, :])
                spot = pl.ds(n * 520 + tile * 64 + y, 8, stride=8)
                out[spot, :] = norm[spot, :] * value
            both = jnp.where(
                take_left,
                jnp.broadcast_to(sf[start + 17 : start + 18, :], (8, 128)),
                jnp.broadcast_to(sf[start + 16 : start + 17, :], (8, 128)),
            )
            place = ((n * 8 + y) * NT + 8) * 8
            value = jnp.where(edge, roll(both, -6), main[place : place + 8, :])
            spot = n * 520 + 512 + y
            out[spot : spot + 1, :] = norm[spot : spot + 1, :] * value[0:1, :]


def call(body, shapes, specs, scratch=(), cost=None):
    return pl.pallas_call(
        body,
        out_shape=[jax.ShapeDtypeStruct((n, 128), F32) for n in shapes],
        in_specs=specs,
        out_specs=[VM] * len(shapes),
        scratch_shapes=list(scratch),
        cost_estimate=cost,
        compiler_params=pltpu.CompilerParams(vmem_limit_bytes=32 << 20),
    )


def estimate(flops, bytes_accessed):
    return pl.CostEstimate(flops=flops, bytes_accessed=bytes_accessed, transcendentals=0)


def on_device(
    obs_resid, obs_cell, azimuth, gate_count, kappa_xx, kappa_yy, kappa_shear, norm_scale
):
    rows, columns = lax.axis_size("row"), lax.axis_size("col")
    pos = jnp.stack([lax.axis_index("row"), lax.axis_index("col")]).astype(jnp.int32)
    flat = lambda a: a.reshape(-1, 128)
    kt_rows = 3 * 8 * LV
    pay_rows = 96 + 4 * 3 * LV
    msg_rows = NM * 8 + 88
    pay_a, pay_b, kt = call(
        prepare, (pay_rows, pay_rows, kt_rows), [SM, SM] + [VM] * 6
    )(
        pos,
        gate_count,
        flat(obs_resid),
        flat(obs_cell),
        flat(azimuth),
        flat(kappa_xx),
        flat(kappa_yy),
        flat(kappa_shear),
    )
    rec_b = lax.ppermute(pay_b, "row", pairs(rows, 1))
    rec_a = lax.ppermute(pay_a, "row", pairs(rows, 0))
    work = (
        pltpu.VMEM((8 * LV, KC), BF16),
        pltpu.VMEM((256 * SPLITS, KC), BF16),
        pltpu.VMEM((64 + 64 * SPLITS, 128), F32),
    )
    u, v = call(
        own_wind, (8 * LV, 8 * LV), [VM], work, estimate(3_000_000_000, 2_000_000)
    )(pay_a[0:96])
    hu, hv, kh, sw, sk, msg_c, msg_d = call(
        edges,
        (10 * LV, 10 * LV, 7 * 3 * LV, 36 * 24, 45 * 24, msg_rows, msg_rows),
        [SM] + [VM] * 5,
        work,
    )(pos, rec_a, rec_b, u, v, kt)
    rec_c = lax.ppermute(msg_c, "col", pairs(columns, 0))
    rec_d = lax.ppermute(msg_d, "col", pairs(columns, 1))
    (main,) = call(
        lambda *refs: middle(rows, *refs),
        (16 * LV,),
        [SM] + [VM] * 6,
        (),
        estimate(3_000_000_000, 4_000_000),
    )(pos, u, v, hu, hv, kt, kh)
    (out,) = call(
        lambda *refs: finish(rows, columns, *refs),
        (2 * 65 * 8,),
        [SM] + [VM] * 6,
        (
            pltpu.VMEM((36 * 24, 128), F32),
            pltpu.VMEM((45 * 24, 128), F32),
            pltpu.VMEM((24, 128), F32),
            pltpu.VMEM((16 * 24, 128), F32),
        ),
    )(pos, rec_c, rec_d, sw, sk, main, flat(norm_scale))
    return out.reshape(norm_scale.shape)


def solution(mesh):
    in_specs = (
        P("row", "col"),
        P("row", "col"),
        P("row", "col"),
        P("row", "col"),
        P(None, "row", "col"),
        P(None, "row", "col"),
        P(None, "row", "col"),
        P(None, None, "row", "col"),
    )
    out_specs = P(None, None, "row", "col")
    return jax.shard_map(
        on_device, mesh=mesh, in_specs=in_specs, out_specs=out_specs, check_vma=False
    )
```

```python
import jax
import jax.numpy as jnp
from jax import lax
from jax.experimental import pallas as pl
from jax.experimental.pallas import tpu as pltpu
from jax.sharding import PartitionSpec as P

STEPS = 4
NT = 8
F32 = jnp.float32
BF16 = jnp.bfloat16
KC = 1024
SPLITS = 2
NQ = 81
NM = NQ // 3
GROUP = 2
PAY = 96 + 12 * 64 + 16
TAB = 320 + 64 * SPLITS
OWN = 8 * 64 + 16
HALO = 5 * 64 + 16
HB = pl.BlockSpec(memory_space=pltpu.HBM)
VM = pl.BlockSpec(memory_space=pltpu.VMEM)
SM = pl.BlockSpec(memory_space=pltpu.SMEM)


def pairs(size, first):
    out = []
    for i in range(first, size - 1, 2):
        out += [(i, i + 1), (i + 1, i)]
    return out


def roll(x, by):
    by = by % 128
    return x if by == 0 else pltpu.roll(x, by, 1)


def at(ref, i):
    return ref[pl.ds(pl.multiple_of(i * 8, 8), 8), :]


def wide(ref, row):
    return jnp.broadcast_to(ref[row : row + 1, :], (8, 128))


def lanes():
    return lax.broadcasted_iota(jnp.int32, (8, 128), 1)


def sublanes():
    return lax.broadcasted_iota(jnp.int32, (8, 128), 0)


def prepare(pos, gate, resid_h, cell_h, azimuth_h, kxx_h, kyy_h, ksh_h, pay_a, pay_b, kt,
            resid, cell, azimuth, kxx, kyy, ksh, sems):
    copies = []
    for i, (src, dst) in enumerate(
        (
            (resid_h, resid),
            (cell_h, cell),
            (azimuth_h, azimuth),
            (kxx_h, kxx),
            (kyy_h, kyy),
            (ksh_h, ksh),
        )
    ):
        copies.append(pltpu.make_async_copy(src, dst, sems.at[i]))
        copies[-1].start()
    odd = (pos[0] & 1) == 1
    slot = lax.broadcasted_iota(jnp.int32, (32, 128), 0) * 128 + lax.broadcasted_iota(
        jnp.int32, (32, 128), 1
    )
    for copy in copies[:3]:
        copy.wait()
    weight = jnp.where(slot < gate[0, 0], resid[...], 0.0)
    angle = azimuth[...]
    wu = weight * jnp.sin(angle)
    wv = weight * jnp.cos(angle)
    cf = cell[...].astype(F32)
    for pay in (pay_a, pay_b):
        pay[0:32, :] = wu
        pay[32:64, :] = wv
        pay[64:96, :] = cf
        pay[876:880, :] = jnp.zeros((4, 128), F32)
    for copy in copies[3:]:
        copy.wait()

    def entries(get):
        xx, yy = get(kxx), get(kyy)
        return xx, get(ksh) * jnp.sqrt(xx * yy), yy

    for tile in range(NT):
        rows = []
        for y in range(8):
            rows.append(entries(lambda ref: ref[pl.ds(tile * 64 + y, 8, stride=8), :]))
            for q in range(3):
                start = (q * 8 + y) * 64 + tile * 8
                kt[start : start + 8, :] = rows[y][q]
        for i in range(4):
            for q in range(3):
                start = 96 + (i * 3 + q) * 64 + tile * 8
                low, high = rows[i][q], rows[i + 4][q]
                pay_a[start : start + 8, :] = jnp.where(odd, low, high)
                pay_b[start : start + 8, :] = jnp.where(odd, high, low)
    last = entries(lambda ref: ref[512:520, :])
    for q in range(3):
        kt[1536 + q * 8 : 1544 + q * 8, :] = last[q]
        for i in range(4):
            start = 864 + i * 3 + q
            low, high = last[q][i : i + 1, :], last[q][i + 4 : i + 5, :]
            pay_a[start : start + 1, :] = jnp.where(odd, low, high)
            pay_b[start : start + 1, :] = jnp.where(odd, high, low)


def scatter(jobs, hots, vals, tab, out_u, out_v):
    first = lax.broadcasted_iota(jnp.int32, (16, 128), 0).astype(F32)
    iota = [(first + 16.0 * b).astype(BF16) for b in range(8)]
    one = jnp.full((16, 128), 1, BF16)
    zero = jnp.full((16, 128), 0, BF16)
    per = KC // 128
    chunks = 4096 // KC
    for job, (wu, wv, cf, shift, ny, _) in enumerate(jobs):
        cell = cf.astype(jnp.int32)
        level = lax.shift_right_logical(cell, 10)
        row = (lax.shift_right_logical(cell, 7) & 7) - shift
        lf = level.astype(F32)
        index = [jnp.where((row == y) & (level < 64), lf, -1.0) for y in range(ny)]
        index += [jnp.full((32, 128), -1.0, F32)] * (8 - ny)
        index.append(jnp.where((level == 64) & (row < ny), row.astype(F32), -1.0))
        index.append((cell & 127).astype(F32))
        for value in (wu, wv):
            for s in range(SPLITS):
                top = value.astype(BF16).astype(F32)
                value = value - top
                index.append(top)
        for k, value in enumerate(index):
            start = job * TAB + k * 32
            tab[start : start + 32, :] = value

    def build(job, c):
        ny = jobs[job][4]
        for j in range(per):

            def spread(k):
                i = job * TAB + k * 32 + c * per + j
                return jnp.broadcast_to(tab[i : i + 1, :], (16, 128)).astype(BF16)

            rows = []
            for y in range(ny):
                index = spread(y)
                for b in range(4):
                    rows.append(jnp.where(iota[b] == index, one, zero))
            rows.append(jnp.where(iota[0] == spread(8), one, zero))
            hot[job, c, j] = jnp.concatenate(rows, axis=0)
            col = spread(9)
            parts = [spread(10 + k) for k in range(2 * SPLITS)]
            hits = [iota[b] == col for b in range(8)]
            val[job, c, j] = jnp.concatenate(
                [
                    jnp.where(hit, parts[n * SPLITS + s], zero)
                    for s in range(SPLITS)
                    for n in range(2)
                    for hit in hits
                ],
                axis=0,
            )

    def multiply(job, c):
        ny, base = jobs[job][4:]
        count = ny * 64 + 16
        total = None
        left = jnp.concatenate([hot[job, c, j] for j in range(per)], axis=1)
        for s in range(SPLITS):
            part = lax.dot_general(
                left,
                jnp.concatenate(
                    [val[job, c, j][s * 256 : s * 256 + 256] for j in range(per)], axis=1
                ),
                (((1,), (1,)), ((), ())),
                preferred_element_type=F32,
            )
            total = part if total is None else total + part
        for ref, part in ((out_u, total[:, 0:128]), (out_v, total[:, 128:256])):
            if c > 0:
                part = part + ref[base : base + count, :]
            ref[base : base + count, :] = part

    hot, val = {}, {}
    steps = [(job, c) for job in range(len(jobs)) for c in range(chunks)]
    build(*steps[0])
    for now, later in zip(steps, steps[1:] + [None]):
        if later is not None:
            build(*later)
        multiply(*now)


def wind_at(own, halo, row, tile):
    if 0 <= row < 8:
        return wide(own, 512 + row) if tile is None else at(own, row * NT + tile)
    base, row = (0, row + 5) if row < 0 else (HALO, row - 8)
    if tile is None:
        return wide(halo, base + 320 + row)
    return at(halo, base // 8 + row * NT + tile)


def kappa_at(kt, halo, q, row, tile):
    if 0 <= row < 8:
        row = q * 8 + row
        return wide(kt, 1536 + row) if tile is None else at(kt, row * NT + tile)
    row = ((row + 4) if row < 0 else row - 4) * 3 + q
    return wide(halo, 1344 + row) if tile is None else at(halo, row * NT + tile)


def strip(get, ref, index):
    lane = lanes()
    left_slot = lane // 16
    right_slot = ((lane + 4) % 128) // 16
    left = right = None
    for j in range(8):
        moved = roll(get(j), 16 * j + 6)
        left = moved if j == 0 else jnp.where(left_slot == j, moved, left)
        right = moved if j == 0 else jnp.where(right_slot == j, moved, right)
    whole = get(None)
    last = jnp.where(sublanes() == 2, whole, roll(whole, 6))
    start = index * 24
    ref[start : start + 8, :] = left
    ref[start + 8 : start + 16, :] = right
    ref[start + 16 : start + 24, :] = last


def own_part(obs, kt, u, v, sw, sk, hot_a, hot_b, val_a, val_b, tab):
    job = (obs[0:32, :], obs[32:64, :], obs[64:96, :], 0, 8, 0)
    scatter([job], (hot_a, hot_b), (val_a, val_b), tab, u, v)
    for y in range(8):
        for n, ref in enumerate((u, v)):
            strip(lambda t: wind_at(ref, None, y, t), sw, n * 8 + y)
        for q in range(3):
            strip(lambda t: kappa_at(kt, None, q, y, t), sk, q * 8 + y)


def strip_place(k, sw, sk, tw, tk):
    if k < 36:
        n, row = k // 18, k % 18 - 5
        if 0 <= row < 8:
            return sw, n * 8 + row
        return tw, n * 10 + ((row + 5) if row < 0 else row - 3)
    q, row = (k - 36) // 15, (k - 36) % 15 - 4
    if 0 <= row < 8:
        return sk, q * 8 + row
    return tk, q * 7 + ((row + 4) if row < 0 else row - 4)


def edges(pos, rec_a, rec_b, sw, sk, hu, hv, kh, tw, tk, msg_c, msg_d,
          hot_a, hot_b, val_a, val_b, tab):
    odd = (pos[0] & 1) == 1
    for q in range(3):
        for j in range(7):
            row, one, two = (j, rec_a, rec_b) if j < 4 else (j - 4, rec_b, rec_a)
            src = 96 + (row * 3 + q) * 64
            dst = (j * 3 + q) * 64
            kh[dst : dst + 64, :] = jnp.where(odd, one[src : src + 64, :], two[src : src + 64, :])
            src, dst = 864 + row * 3 + q, 1344 + j * 3 + q
            kh[dst : dst + 1, :] = jnp.where(odd, one[src : src + 1, :], two[src : src + 1, :])
    kh[1365:1368, :] = jnp.zeros((3, 128), F32)
    jobs = []
    for side in range(2):
        one, two = (rec_a, rec_b) if side == 0 else (rec_b, rec_a)
        part = jnp.where(odd, one[0:96, :], two[0:96, :])
        jobs.append((part[0:32], part[32:64], part[64:96], 3 - 3 * side, 5, side * HALO))
    scatter(jobs, (hot_a, hot_b), (val_a, val_b), tab, hu, hv)
    for i in range(10):
        row = i - 5 if i < 5 else i + 3
        for n, ref in enumerate((hu, hv)):
            strip(lambda t: wind_at(None, ref, row, t), tw, n * 10 + i)
    for i in range(7):
        row = i - 4 if i < 4 else i + 4
        for q in range(3):
            strip(lambda t: kappa_at(None, kh, q, row, t), tk, q * 7 + i)
    fifth = lanes() % 16
    odd_col = (pos[1] & 1) == 1
    for i in range(NM):
        packed = []
        for t in range(3):
            ref, index = strip_place(3 * i + t, sw, sk, tw, tk)
            left = ref[index * 24 : index * 24 + 8, :]
            packed.append((roll(left, 5 * t), roll(left, 5 * t - 5)))
            row = NM * 8 + 3 * i + t
            last = ref[index * 24 + 16 : index * 24 + 17, :]
            msg_c[row : row + 1, :] = last
            msg_d[row : row + 1, :] = last
        right_edge, left_edge = (
            jnp.where(fifth < 6, packed[0][e], jnp.where(fifth < 11, packed[1][e], packed[2][e]))
            for e in range(2)
        )
        msg_c[i * 8 : i * 8 + 8, :] = jnp.where(odd_col, left_edge, right_edge)
        msg_d[i * 8 : i * 8 + 8, :] = jnp.where(odd_col, right_edge, left_edge)
    fill = NM * 8 + NQ
    for msg in (msg_c, msg_d):
        msg[fill : fill + 7, :] = jnp.zeros((7, 128), F32)


def derive(wind, low, high, mask, put):
    for row in range(-4, 12):
        side = low if row < 0 else high if row > 7 else None
        across = []
        along = []
        for n in range(2):
            here = wind(n, row)
            across.append(roll(here, -1) - roll(here, 1))
            along.append(wind(n, row + 1) - wind(n, row - 1))
        scale = 0.5 if side is None else 0.5 * side
        if mask is not None:
            scale = scale * mask
        put(0, row, scale * (along[0] - across[1]))
        put(1, row, -scale * (across[0] + along[1]))


def advance(more, field, kappa, high, mask, put):
    before = {}
    here = [field(n, -more - 1) for n in range(2)]
    for row in range(-more - 1, 8 + more):
        xx, xy, yy = (kappa(q, row) for q in range(3))
        for n in range(2):
            below = field(n, row + 1)
            gx = roll(here[n], -1) - here[n]
            gy = below - here[n]
            hx = xx * gx + xy * gy
            hy = xy * gx + yy * gy
            if row >= -more:
                value = here[n] - (roll(hx, 1) - hx + (before[n] - hy))
                if row > 7:
                    value = value * high
                if mask is not None:
                    value = value * mask
                put(n, row, value)
            before[n] = hy
            here[n] = below


def slab(ref, tiles, tile):
    def get(n, row):
        return at(ref, (n * 16 + row + 4) * tiles + tile)

    def put(n, row, value):
        start = ((n * 16 + row + 4) * tiles + tile) * 8
        ref[pl.ds(pl.multiple_of(start, 8), 8), :] = value

    return get, put


def ends(pos, size):
    low = jnp.where(pos[0] == 0, 0.0, 1.0).astype(F32)
    high = jnp.where(pos[0] == size - 1, 0.0, 1.0).astype(F32)
    return low, high


def middle(size, pos, u, v, hu, hv, kt, kh, main, fa, fb):
    low, high = ends(pos, size)
    wind_refs = ((u, hu), (v, hv))

    def stage(step):
        def body(g, _):
            for k in range(GROUP):
                tile = g * GROUP + k
                if step < 0:
                    put = slab(fa, NT, tile)[1]
                    derive(lambda n, row: wind_at(*wind_refs[n], row, tile), low, high, None, put)
                    continue
                src, dst = (fa, fb) if step % 2 == 0 else (fb, fa)
                put = slab(dst, NT, tile)[1]
                if step == STEPS - 1:

                    def put(n, row, value):
                        start = pl.multiple_of(((n * 8 + row) * NT + tile) * 8, 8)
                        main[pl.ds(start, 8), :] = value

                advance(
                    STEPS - 1 - step,
                    slab(src, NT, tile)[0],
                    lambda q, row: kappa_at(kt, kh, q, row, tile),
                    high,
                    None,
                    put,
                )
            return 0

        lax.fori_loop(0, NT // GROUP, body, 0)

    for step in range(-1, STEPS):
        stage(step)


def finish(
    rows, columns, pos, rec_c, rec_d, sw, sk, tw, tk, main, norm, out, mw, mk, masks, fa, fb
):
    low, high = ends(pos, rows)
    odd_col = (pos[1] & 1) == 1
    lane = lanes()
    fifth = lane % 16
    sub = sublanes()
    take_left = (fifth >= 1) & (fifth <= 5)
    take_right = (fifth >= 6) & (fifth <= 10)
    take_last = (take_left & (sub == 0)) | (take_right & (sub == 1))
    for k in range(NQ):
        i, t = k // 3, k % 3
        a = rec_c[i * 8 : i * 8 + 8, :]
        b = rec_d[i * 8 : i * 8 + 8, :]
        from_left = roll(jnp.where(odd_col, a, b), -5 * t)
        from_right = roll(jnp.where(odd_col, b, a), 5 - 5 * t)
        row = NM * 8 + k
        last = jnp.where((sub == 0) == odd_col, wide(rec_c, row), wide(rec_d, row))
        src, index = strip_place(k, sw, sk, tw, tk)
        here = index * 24
        dst, start = (mw, k * 24) if k < 36 else (mk, (k - 36) * 24)
        dst[start : start + 8, :] = jnp.where(take_left, from_left, src[here : here + 8, :])
        dst[start + 8 : start + 16, :] = jnp.where(
            take_right, from_right, src[here + 8 : here + 16, :]
        )
        dst[start + 16 : start + 24, :] = jnp.where(take_last, last, src[here + 16 : here + 24, :])
    west = jnp.where(pos[1] == 0, 0.0, 1.0).astype(F32)
    east = jnp.where(pos[1] == columns - 1, 0.0, 1.0).astype(F32)
    left_mask = jnp.where(fifth < 6, west, 1.0)
    right_mask = jnp.where((fifth >= 6) & (fifth < 12), east, 1.0)
    masks[0:8, :] = left_mask
    masks[8:16, :] = right_mask
    masks[16:24, :] = jnp.where(sub == 0, left_mask, jnp.where(sub == 1, right_mask, 1.0))
    for step in range(-1, STEPS):
        for tile in range(3):
            mask = masks[tile * 8 : tile * 8 + 8, :]
            src, dst = (fa, fb) if step % 2 == 0 else (fb, fa)
            put = slab(dst, 3, tile)[1]
            if step < 0:
                derive(
                    lambda n, row: at(mw, (n * 18 + row + 5) * 3 + tile), low, high, mask, put
                )
            else:
                advance(
                    STEPS - 1 - step,
                    slab(src, 3, tile)[0],
                    lambda q, row: at(mk, (q * 15 + row + 4) * 3 + tile),
                    high,
                    mask,
                    put,
                )
    done = fb if STEPS % 2 == 1 else fa
    edge = (lane < 5) | (lane >= 123)
    for n in range(2):
        for y in range(8):
            left, right, last = (slab(done, 3, tile)[0](n, y) for tile in range(3))
            both = jnp.where(take_left, right, left)
            for tile in range(NT):
                place = ((n * 8 + y) * NT + tile) * 8
                value = jnp.where(edge, roll(both, -(16 * tile + 6)), main[place : place + 8, :])
                spot = pl.ds(n * 520 + tile * 64 + y, 8, stride=8)
                out[spot, :] = norm[spot, :] * value
            both = roll(jnp.where(take_left[0:1], last[1:2], last[0:1]), -6)
            value = jnp.where(edge[0:1], both, last[2:3])
            spot = n * 520 + 512 + y
            out[spot : spot + 1, :] = norm[spot : spot + 1, :] * value


def call(body, shapes, specs, scratch=(), cost=None):
    return pl.pallas_call(
        body,
        out_shape=[jax.ShapeDtypeStruct((n, 128), F32) for n in shapes],
        in_specs=specs,
        out_specs=[VM] * len(shapes),
        scratch_shapes=list(scratch),
        cost_estimate=cost,
        compiler_params=pltpu.CompilerParams(vmem_limit_bytes=32 << 20),
    )


def estimate(flops, bytes_accessed):
    return pl.CostEstimate(flops=flops, bytes_accessed=bytes_accessed, transcendentals=0)


def on_device(
    obs_resid, obs_cell, azimuth, gate_count, kappa_xx, kappa_yy, kappa_shear, norm_scale
):
    rows, columns = lax.axis_size("row"), lax.axis_size("col")
    pos = jnp.stack([lax.axis_index("row"), lax.axis_index("col")]).astype(jnp.int32)
    flat = lambda a: a.reshape(-1, 128)
    buffers = lambda *shapes: tuple(pltpu.VMEM((n, 128), t) for n, t in shapes)
    pay_a, pay_b, kt = call(
        prepare,
        (PAY, PAY, 24 * 64 + 24),
        [SM, SM] + [HB] * 6,
        buffers((32, F32), (32, jnp.int32), (32, F32), (520, F32), (520, F32), (520, F32))
        + (pltpu.SemaphoreType.DMA((6,)),),
    )(
        pos,
        gate_count,
        *(
            pltpu.with_memory_space_constraint(flat(a), pltpu.HBM)
            for a in (obs_resid, obs_cell, azimuth, kappa_xx, kappa_yy, kappa_shear)
        ),
    )
    rec_b = lax.ppermute(pay_b, "row", pairs(rows, 1))
    rec_a = lax.ppermute(pay_a, "row", pairs(rows, 0))
    work = (
        pltpu.VMEM((KC // 128, OWN, 128), BF16),
        pltpu.VMEM((KC // 128, OWN, 128), BF16),
        pltpu.VMEM((KC // 128, 256 * SPLITS, 128), BF16),
        pltpu.VMEM((KC // 128, 256 * SPLITS, 128), BF16),
        pltpu.VMEM((2 * TAB, 128), F32),
    )
    u, v, sw, sk = call(
        own_part,
        (OWN, OWN, 16 * 24, 24 * 24),
        [VM] * 2,
        work,
        estimate(3_000_000_000, 2_000_000),
    )(pay_a[0:96], kt)
    hu, hv, kh, tw, tk, msg_c, msg_d = call(
        edges,
        (2 * HALO, 2 * HALO, 21 * 64 + 24, 20 * 24, 21 * 24, NM * 8 + 88, NM * 8 + 88),
        [SM] + [VM] * 4,
        work,
    )(pos, rec_a, rec_b, sw, sk)
    rec_c = lax.ppermute(msg_c, "col", pairs(columns, 0))
    rec_d = lax.ppermute(msg_d, "col", pairs(columns, 1))
    (main,) = call(
        lambda *refs: middle(rows, *refs),
        (16 * 64,),
        [SM] + [VM] * 6,
        buffers((32 * 64, F32), (32 * 64, F32)),
        estimate(3_000_000_000, 4_000_000),
    )(pos, u, v, hu, hv, kt, kh)
    (out,) = call(
        lambda *refs: finish(rows, columns, *refs),
        (2 * 65 * 8,),
        [SM] + [VM] * 8,
        buffers((36 * 24, F32), (45 * 24, F32), (24, F32), (32 * 24, F32), (32 * 24, F32)),
    )(pos, rec_c, rec_d, sw, sk, tw, tk, main, flat(norm_scale))
    return out.reshape(norm_scale.shape)


def solution(mesh):
    in_specs = (
        P("row", "col"),
        P("row", "col"),
        P("row", "col"),
        P("row", "col"),
        P(None, "row", "col"),
        P(None, "row", "col"),
        P(None, "row", "col"),
        P(None, None, "row", "col"),
    )
    out_specs = P(None, None, "row", "col")
    return jax.shard_map(
        on_device, mesh=mesh, in_specs=in_specs, out_specs=out_specs, check_vma=False
    )
```

```python
import jax
import jax.numpy as jnp
from jax import lax
from jax.experimental import pallas as pl
from jax.experimental.pallas import tpu as pltpu
from jax.sharding import PartitionSpec as P


STEPS = 4
NT = 8
F32 = jnp.float32
BF16 = jnp.bfloat16
KC = 1024
SPLITS = 2
NQ = 81
NM = NQ // 3
MSG = NM * 8 + 16
GROUP = 8
PAY = 96 + 12 * 64 + 16
TAB = 320 + 64 * SPLITS
OWN = 8 * 64 + 16
HALO = 5 * 64 + 16
HB = pl.BlockSpec(memory_space=pltpu.HBM)
VM = pl.BlockSpec(memory_space=pltpu.VMEM)
SM = pl.BlockSpec(memory_space=pltpu.SMEM)


def pairs(size, first):
    out = []
    for i in range(first, size - 1, 2):
        out += [(i, i + 1), (i + 1, i)]
    return out


def roll(x, by):
    by = by % 128
    return x if by == 0 else pltpu.roll(x, by, 1)


def at(ref, i):
    return ref[pl.ds(pl.multiple_of(i * 8, 8), 8), :]


def wide(ref, row):
    return jnp.broadcast_to(ref[row : row + 1, :], (8, 128))


def lanes():
    return lax.broadcasted_iota(jnp.int32, (8, 128), 1)


def sublanes():
    return lax.broadcasted_iota(jnp.int32, (8, 128), 0)


def prepare(pos, gate, resid_h, cell_h, azimuth_h, kxx_h, kyy_h, ksh_h, pay_a, pay_b, kt,
            resid, cell, azimuth, kxx, kyy, ksh, sems):
    copies = []
    for i, (src, dst) in enumerate(
        (
            (resid_h, resid),
            (cell_h, cell),
            (azimuth_h, azimuth),
            (kxx_h, kxx),
            (kyy_h, kyy),
            (ksh_h, ksh),
        )
    ):
        copies.append(pltpu.make_async_copy(src, dst, sems.at[i]))
        copies[-1].start()
    odd = (pos[0] & 1) == 1
    slot = lax.broadcasted_iota(jnp.int32, (32, 128), 0) * 128 + lax.broadcasted_iota(
        jnp.int32, (32, 128), 1
    )
    for copy in copies[:3]:
        copy.wait()
    weight = jnp.where(slot < gate[0, 0], resid[...], 0.0)
    angle = azimuth[...]
    wu = weight * jnp.sin(angle)
    wv = weight * jnp.cos(angle)
    cf = cell[...].astype(F32)
    for pay in (pay_a, pay_b):
        pay[0:32, :] = wu
        pay[32:64, :] = wv
        pay[64:96, :] = cf
        pay[876:880, :] = jnp.zeros((4, 128), F32)
    for copy in copies[3:]:
        copy.wait()

    def entries(get):
        xx, yy = get(kxx), get(kyy)
        return xx, get(ksh) * jnp.sqrt(xx * yy), yy

    for tile in range(NT):
        rows = []
        for y in range(8):
            rows.append(entries(lambda ref: ref[pl.ds(tile * 64 + y, 8, stride=8), :]))
            for q in range(3):
                start = (q * 8 + y) * 64 + tile * 8
                kt[start : start + 8, :] = rows[y][q]
        for i in range(4):
            for q in range(3):
                start = 96 + (i * 3 + q) * 64 + tile * 8
                low, high = rows[i][q], rows[i + 4][q]
                pay_a[start : start + 8, :] = jnp.where(odd, low, high)
                pay_b[start : start + 8, :] = jnp.where(odd, high, low)
    last = entries(lambda ref: ref[512:520, :])
    for q in range(3):
        kt[1536 + q * 8 : 1544 + q * 8, :] = last[q]
        for i in range(4):
            start = 864 + i * 3 + q
            low, high = last[q][i : i + 1, :], last[q][i + 4 : i + 5, :]
            pay_a[start : start + 1, :] = jnp.where(odd, low, high)
            pay_b[start : start + 1, :] = jnp.where(odd, high, low)


def scatter(jobs, tab, out_u, out_v):
    first = lax.broadcasted_iota(jnp.int32, (16, 128), 0).astype(F32)
    iota = [(first + 16.0 * b).astype(BF16) for b in range(8)]
    one = jnp.full((16, 128), 1, BF16)
    zero = jnp.full((16, 128), 0, BF16)
    per = KC // 128
    chunks = 4096 // KC
    for job, (wu, wv, cf, shift, ny, _) in enumerate(jobs):
        cell = cf.astype(jnp.int32)
        level = lax.shift_right_logical(cell, 10)
        row = (lax.shift_right_logical(cell, 7) & 7) - shift
        lf = level.astype(F32)
        index = [jnp.where((row == y) & (level < 64), lf, -1.0) for y in range(ny)]
        index += [jnp.full((32, 128), -1.0, F32)] * (8 - ny)
        index.append(jnp.where((level == 64) & (row < ny), row.astype(F32), -1.0))
        index.append((cell & 127).astype(F32))
        for value in (wu, wv):
            for _ in range(SPLITS):
                top = value.astype(BF16).astype(F32)
                value = value - top
                index.append(top)
        for k, value in enumerate(index):
            start = job * TAB + k * 32
            tab[start : start + 32, :] = value

    def build(job, c):
        ny = jobs[job][4]
        for j in range(per):

            def spread(k):
                i = job * TAB + k * 32 + c * per + j
                return jnp.broadcast_to(tab[i : i + 1, :], (16, 128)).astype(BF16)

            rows = []
            for y in range(ny):
                index = spread(y)
                for b in range(4):
                    rows.append(jnp.where(iota[b] == index, one, zero))
            rows.append(jnp.where(iota[0] == spread(8), one, zero))
            hot[job, c, j] = jnp.concatenate(rows, axis=0)
            col = spread(9)
            parts = [spread(10 + k) for k in range(2 * SPLITS)]
            hits = [iota[b] == col for b in range(8)]
            val[job, c, j] = jnp.concatenate(
                [
                    jnp.where(hit, parts[n * SPLITS + s], zero)
                    for s in range(SPLITS)
                    for n in range(2)
                    for hit in hits
                ],
                axis=0,
            )

    def multiply(job, c):
        ny, base = jobs[job][4:]
        count = ny * 64 + 16
        total = None
        left = jnp.concatenate([hot[job, c, j] for j in range(per)], axis=1)
        for s in range(SPLITS):
            part = lax.dot_general(
                left,
                jnp.concatenate(
                    [val[job, c, j][s * 256 : s * 256 + 256] for j in range(per)], axis=1
                ),
                (((1,), (1,)), ((), ())),
                preferred_element_type=F32,
            )
            total = part if total is None else total + part
        for ref, part in ((out_u, total[:, 0:128]), (out_v, total[:, 128:256])):
            if c > 0:
                part = part + ref[base : base + count, :]
            ref[base : base + count, :] = part

    hot, val = {}, {}
    steps = [(job, c) for job in range(len(jobs)) for c in range(chunks)]
    build(*steps[0])
    for now, later in zip(steps, steps[1:] + [None]):
        if later is not None:
            build(*later)
        multiply(*now)


def wind_at(own, halo, row, tile):
    if 0 <= row < 8:
        return wide(own, 512 + row) if tile is None else at(own, row * NT + tile)
    base, row = (0, row + 5) if row < 0 else (HALO, row - 8)
    if tile is None:
        return wide(halo, base + 320 + row)
    return at(halo, base // 8 + row * NT + tile)


def kappa_at(kt, halo, q, row, tile):
    if 0 <= row < 8:
        row = q * 8 + row
        return wide(kt, 1536 + row) if tile is None else at(kt, row * NT + tile)
    row = ((row + 4) if row < 0 else row - 4) * 3 + q
    return wide(halo, 1344 + row) if tile is None else at(halo, row * NT + tile)


def strip(get, ref, index):
    lane = lanes()
    left_slot = lane // 16
    right_slot = ((lane + 4) % 128) // 16
    left = right = None
    for j in range(8):
        moved = roll(get(j), 16 * j + 6)
        left = moved if j == 0 else jnp.where(left_slot == j, moved, left)
        right = moved if j == 0 else jnp.where(right_slot == j, moved, right)
    whole = get(None)
    last = jnp.where(sublanes() == 2, whole, roll(whole, 6))
    start = index * 24
    ref[start : start + 8, :] = left
    ref[start + 8 : start + 16, :] = right
    ref[start + 16 : start + 24, :] = last


def own_part(obs, kt, u, v, sw, sk, tab):
    job = (obs[0:32, :], obs[32:64, :], obs[64:96, :], 0, 8, 0)
    scatter([job], tab, u, v)
    for y in range(8):
        for n, ref in enumerate((u, v)):
            strip(lambda t: wind_at(ref, None, y, t), sw, n * 8 + y)
        for q in range(3):
            strip(lambda t: kappa_at(kt, None, q, y, t), sk, q * 8 + y)


def strip_place(k, sw, sk, tw, tk):
    if k < 36:
        n, row = k // 18, k % 18 - 5
        if 0 <= row < 8:
            return sw, n * 8 + row
        return tw, n * 10 + ((row + 5) if row < 0 else row - 3)
    q, row = (k - 36) // 15, (k - 36) % 15 - 4
    if 0 <= row < 8:
        return sk, q * 8 + row
    return tk, q * 7 + ((row + 4) if row < 0 else row - 4)


def near(pos, rec_a, u, v, tab):
    job = (rec_a[0:32, :], rec_a[32:64, :], rec_a[64:96, :], (pos[0] & 1) * 3, 5, 0)
    scatter([job], tab, u, v)


def edges(pos, rec_a, rec_b, au, av, sw, sk, hu, hv, kh, tw, tk, msg_c, msg_d, bu, bv, last, tab):
    odd = (pos[0] & 1) == 1
    for q in range(3):
        for j in range(7):
            row, one, two = (j, rec_a, rec_b) if j < 4 else (j - 4, rec_b, rec_a)
            src = 96 + (row * 3 + q) * 64
            dst = (j * 3 + q) * 64
            kh[dst : dst + 64, :] = jnp.where(odd, one[src : src + 64, :], two[src : src + 64, :])
            src, dst = 864 + row * 3 + q, 1344 + j * 3 + q
            kh[dst : dst + 1, :] = jnp.where(odd, one[src : src + 1, :], two[src : src + 1, :])
    kh[1365:1368, :] = jnp.zeros((3, 128), F32)
    job = (rec_b[0:32, :], rec_b[32:64, :], rec_b[64:96, :], 3 - (pos[0] & 1) * 3, 5, 0)
    scatter([job], tab, bu, bv)
    for out, one, two in ((hu, au, bu), (hv, av, bv)):
        out[0:HALO, :] = jnp.where(odd, one[...], two[...])
        out[HALO : 2 * HALO, :] = jnp.where(odd, two[...], one[...])
    for i in range(10):
        row = i - 5 if i < 5 else i + 3
        for n, ref in enumerate((hu, hv)):
            strip(lambda t: wind_at(None, ref, row, t), tw, n * 10 + i)
    for i in range(7):
        row = i - 4 if i < 4 else i + 4
        for q in range(3):
            strip(lambda t: kappa_at(None, kh, q, row, t), tk, q * 7 + i)
    fifth = lanes() % 16
    odd_col = (pos[1] & 1) == 1
    for i in range(NM):
        packed = []
        for t in range(3):
            ref, index = strip_place(3 * i + t, sw, sk, tw, tk)
            left = ref[index * 24 : index * 24 + 8, :]
            packed.append((roll(left, 5 * t), roll(left, 5 * t - 5)))
            row = 3 * i + t
            last[row : row + 1, :] = ref[index * 24 + 16 : index * 24 + 17, :]
        right_edge, left_edge = (
            jnp.where(fifth < 6, packed[0][e], jnp.where(fifth < 11, packed[1][e], packed[2][e]))
            for e in range(2)
        )
        msg_c[i * 8 : i * 8 + 8, :] = jnp.where(odd_col, left_edge, right_edge)
        msg_d[i * 8 : i * 8 + 8, :] = jnp.where(odd_col, right_edge, left_edge)
    last[NQ : NQ + 7, :] = jnp.zeros((7, 128), F32)
    slot = lanes() // 16
    for g in range(2):
        packed = last[g * 64 : g * 64 + 8, :]
        for k in range(1, 8 if g == 0 else 3):
            start = g * 64 + k * 8
            packed = jnp.where(slot == k, roll(last[start : start + 8, :], 16 * k), packed)
        start = NM * 8 + g * 8
        msg_c[start : start + 8, :] = packed
        msg_d[start : start + 8, :] = packed


def derive(wind, low, high, mask, put):
    for row in range(-4, 12):
        side = low if row < 0 else high if row > 7 else None
        across = []
        along = []
        for n in range(2):
            here = wind(n, row)
            across.append(roll(here, -1) - roll(here, 1))
            along.append(wind(n, row + 1) - wind(n, row - 1))
        scale = 0.5 if side is None else 0.5 * side
        if mask is not None:
            scale = scale * mask
        put(0, row, scale * (along[0] - across[1]))
        put(1, row, -scale * (across[0] + along[1]))


def advance(more, field, kappa, high, mask, put):
    before = {}
    here = [field(n, -more - 1) for n in range(2)]
    for row in range(-more - 1, 8 + more):
        xx, xy, yy = (kappa(q, row) for q in range(3))
        for n in range(2):
            below = field(n, row + 1)
            gx = roll(here[n], -1) - here[n]
            gy = below - here[n]
            hx = xx * gx + xy * gy
            hy = xy * gx + yy * gy
            if row >= -more:
                value = here[n] - (roll(hx, 1) - hx + (before[n] - hy))
                if row > 7:
                    value = value * high
                if mask is not None:
                    value = value * mask
                put(n, row, value)
            before[n] = hy
            here[n] = below


def slab(ref, tiles, tile):
    def get(n, row):
        return at(ref, (n * 16 + row + 4) * tiles + tile)

    def put(n, row, value):
        start = ((n * 16 + row + 4) * tiles + tile) * 8
        ref[pl.ds(pl.multiple_of(start, 8), 8), :] = value

    return get, put


def ends(pos, size):
    low = jnp.where(pos[0] == 0, 0.0, 1.0).astype(F32)
    high = jnp.where(pos[0] == size - 1, 0.0, 1.0).astype(F32)
    return low, high


def middle(size, pos, u, v, hu, hv, kt, kh, main, fa, fb):
    low, high = ends(pos, size)
    wind_refs = ((u, hu), (v, hv))

    def stage(step):
        def body(g, _):
            for k in range(GROUP):
                tile = g * GROUP + k
                if step < 0:
                    put = slab(fa, NT, tile)[1]
                    derive(lambda n, row: wind_at(*wind_refs[n], row, tile), low, high, None, put)
                    continue
                src, dst = (fa, fb) if step % 2 == 0 else (fb, fa)
                put = slab(dst, NT, tile)[1]
                if step == STEPS - 1:

                    def put(n, row, value):
                        start = pl.multiple_of(((n * 8 + row) * NT + tile) * 8, 8)
                        main[pl.ds(start, 8), :] = value

                advance(
                    STEPS - 1 - step,
                    slab(src, NT, tile)[0],
                    lambda q, row: kappa_at(kt, kh, q, row, tile),
                    high,
                    None,
                    put,
                )
            return 0

        lax.fori_loop(0, NT // GROUP, body, 0)

    for step in range(-1, STEPS):
        stage(step)


def finish(
    rows, columns, pos, rec_c, rec_d, sw, sk, tw, tk, main, norm, out, mw, mk, masks, fa, fb, last_c, last_d
):
    low, high = ends(pos, rows)
    odd_col = (pos[1] & 1) == 1
    lane = lanes()
    fifth = lane % 16
    sub = sublanes()
    take_left = (fifth >= 1) & (fifth <= 5)
    take_right = (fifth >= 6) & (fifth <= 10)
    take_last = (take_left & (sub == 0)) | (take_right & (sub == 1))
    for rec, unpacked in ((rec_c, last_c), (rec_d, last_d)):
        for k in range(11):
            start = NM * 8 + k // 8 * 8
            unpacked[k * 8 : k * 8 + 8, :] = roll(rec[start : start + 8, :], -16 * (k % 8))
    for k in range(NQ):
        i, t = k // 3, k % 3
        a = rec_c[i * 8 : i * 8 + 8, :]
        b = rec_d[i * 8 : i * 8 + 8, :]
        from_left = roll(jnp.where(odd_col, a, b), -5 * t)
        from_right = roll(jnp.where(odd_col, b, a), 5 - 5 * t)
        last = jnp.where((sub == 0) == odd_col, wide(last_c, k), wide(last_d, k))
        src, index = strip_place(k, sw, sk, tw, tk)
        here = index * 24
        dst, start = (mw, k * 24) if k < 36 else (mk, (k - 36) * 24)
        dst[start : start + 8, :] = jnp.where(take_left, from_left, src[here : here + 8, :])
        dst[start + 8 : start + 16, :] = jnp.where(
            take_right, from_right, src[here + 8 : here + 16, :]
        )
        dst[start + 16 : start + 24, :] = jnp.where(take_last, last, src[here + 16 : here + 24, :])
    west = jnp.where(pos[1] == 0, 0.0, 1.0).astype(F32)
    east = jnp.where(pos[1] == columns - 1, 0.0, 1.0).astype(F32)
    left_mask = jnp.where(fifth < 6, west, 1.0)
    right_mask = jnp.where((fifth >= 6) & (fifth < 12), east, 1.0)
    masks[0:8, :] = left_mask
    masks[8:16, :] = right_mask
    masks[16:24, :] = jnp.where(sub == 0, left_mask, jnp.where(sub == 1, right_mask, 1.0))
    for step in range(-1, STEPS):
        for tile in range(3):
            mask = masks[tile * 8 : tile * 8 + 8, :]
            src, dst = (fa, fb) if step % 2 == 0 else (fb, fa)
            put = slab(dst, 3, tile)[1]
            if step < 0:
                derive(
                    lambda n, row: at(mw, (n * 18 + row + 5) * 3 + tile), low, high, mask, put
                )
            else:
                advance(
                    STEPS - 1 - step,
                    slab(src, 3, tile)[0],
                    lambda q, row: at(mk, (q * 15 + row + 4) * 3 + tile),
                    high,
                    mask,
                    put,
                )
    done = fb if STEPS % 2 == 1 else fa
    edge = (lane < 5) | (lane >= 123)
    for n in range(2):
        for y in range(8):
            left, right, last = (slab(done, 3, tile)[0](n, y) for tile in range(3))
            both = jnp.where(take_left, right, left)
            for tile in range(NT):
                place = ((n * 8 + y) * NT + tile) * 8
                value = jnp.where(edge, roll(both, -(16 * tile + 6)), main[place : place + 8, :])
                spot = pl.ds(n * 520 + tile * 64 + y, 8, stride=8)
                out[spot, :] = norm[spot, :] * value
            both = roll(jnp.where(take_left[0:1], last[1:2], last[0:1]), -6)
            value = jnp.where(edge[0:1], both, last[2:3])
            spot = n * 520 + 512 + y
            out[spot : spot + 1, :] = norm[spot : spot + 1, :] * value


def call(body, shapes, specs, scratch=(), cost=None):
    return pl.pallas_call(
        body,
        out_shape=[jax.ShapeDtypeStruct((n, 128), F32) for n in shapes],
        in_specs=specs,
        out_specs=[VM] * len(shapes),
        scratch_shapes=list(scratch),
        cost_estimate=cost,
        compiler_params=pltpu.CompilerParams(vmem_limit_bytes=32 << 20),
    )


def estimate(flops, bytes_accessed):
    return pl.CostEstimate(flops=flops, bytes_accessed=bytes_accessed, transcendentals=0)


def on_device(
    obs_resid, obs_cell, azimuth, gate_count, kappa_xx, kappa_yy, kappa_shear, norm_scale
):
    rows, columns = lax.axis_size("row"), lax.axis_size("col")
    pos = jnp.stack([lax.axis_index("row"), lax.axis_index("col")]).astype(jnp.int32)
    flat = lambda a: a.reshape(-1, 128)
    buffers = lambda *shapes: tuple(pltpu.VMEM((n, 128), t) for n, t in shapes)
    pay_a, pay_b, kt = call(
        prepare,
        (PAY, PAY, 24 * 64 + 24),
        [SM, SM] + [HB] * 6,
        buffers((32, F32), (32, jnp.int32), (32, F32), (520, F32), (520, F32), (520, F32))
        + (pltpu.SemaphoreType.DMA((6,)),),
    )(
        pos,
        gate_count,
        *(
            pltpu.with_memory_space_constraint(flat(a), pltpu.HBM)
            for a in (obs_resid, obs_cell, azimuth, kappa_xx, kappa_yy, kappa_shear)
        ),
    )
    rec_b = lax.ppermute(pay_b, "row", pairs(rows, 1))
    rec_a = lax.ppermute(pay_a, "row", pairs(rows, 0))
    work = buffers((TAB, F32))
    u, v, sw, sk = call(
        own_part,
        (OWN, OWN, 16 * 24, 24 * 24),
        [VM] * 2,
        work,
        estimate(3_000_000_000, 2_000_000),
    )(pay_a[0:96], kt)
    au, av = call(
        near, (HALO, HALO), [SM, VM], work, estimate(3_000_000_000, 2_000_000)
    )(pos, rec_a)
    hu, hv, kh, tw, tk, msg_c, msg_d = call(
        edges,
        (2 * HALO, 2 * HALO, 21 * 64 + 24, 20 * 24, 21 * 24, MSG, MSG),
        [SM] + [VM] * 6,
        buffers((HALO, F32), (HALO, F32), (88, F32)) + work,
    )(pos, rec_a, rec_b, au, av, sw, sk)
    rec_c = lax.ppermute(msg_c, "col", pairs(columns, 0))
    rec_d = lax.ppermute(msg_d, "col", pairs(columns, 1))
    (main,) = call(
        lambda *refs: middle(rows, *refs),
        (16 * 64,),
        [SM] + [VM] * 6,
        buffers((32 * 64, F32), (32 * 64, F32)),
        estimate(3_000_000_000, 4_000_000),
    )(pos, u, v, hu, hv, kt, kh)
    (out,) = call(
        lambda *refs: finish(rows, columns, *refs),
        (2 * 65 * 8,),
        [SM] + [VM] * 8,
        buffers((36 * 24, F32), (45 * 24, F32), (24, F32), (32 * 24, F32), (32 * 24, F32), (88, F32), (88, F32)),
    )(pos, rec_c, rec_d, sw, sk, tw, tk, main, flat(norm_scale))
    return out.reshape(norm_scale.shape)


def solution(mesh):
    in_specs = (
        P("row", "col"),
        P("row", "col"),
        P("row", "col"),
        P("row", "col"),
        P(None, "row", "col"),
        P(None, "row", "col"),
        P(None, "row", "col"),
        P(None, None, "row", "col"),
    )
    out_specs = P(None, None, "row", "col")
    return jax.shard_map(
        on_device, mesh=mesh, in_specs=in_specs, out_specs=out_specs, check_vma=False
    )
```

```python
import jax
import jax.numpy as jnp
from jax import lax
from jax.experimental import pallas as pl
from jax.experimental.pallas import tpu as pltpu
from jax.sharding import PartitionSpec as P


STEPS = 4
NT = 8
F32 = jnp.float32
BF16 = jnp.bfloat16
KC = 1024
SPLITS = 2
NQ = 81
GROUPS = [(list(range(k, k + 3)), 5) for k in range(0, 36, 3)]
GROUPS += [(list(range(k, k + 4)), 4) for k in range(37, NQ, 4)]
NM = len(GROUPS)
MSG = NM * 8 + 16
GROUP = 8
HIGH = [(row, q) for row in range(4, 8) for q in range(3)][1:]
LOW = [(row, q) for row in range(4) for q in range(3)][: len(HIGH)]
UNITS = len(HIGH)
TAIL = 96 + UNITS * 64
PAY = TAIL + 16
PIECES = 4
TAB = 320 + 64 * SPLITS
OWN = 8 * 64 + 16
HALO = 5 * 64 + 16
HB = pl.BlockSpec(memory_space=pltpu.HBM)
VM = pl.BlockSpec(memory_space=pltpu.VMEM)
SM = pl.BlockSpec(memory_space=pltpu.SMEM)


def pairs(size, first):
    out = []
    for i in range(first, size - 1, 2):
        out += [(i, i + 1), (i + 1, i)]
    return out


def roll(x, by):
    by = by % 128
    return x if by == 0 else pltpu.roll(x, by, 1)


def at(ref, i):
    return ref[pl.ds(pl.multiple_of(i * 8, 8), 8), :]


def wide(ref, row):
    return jnp.broadcast_to(ref[row : row + 1, :], (8, 128))


def lanes():
    return lax.broadcasted_iota(jnp.int32, (8, 128), 1)


def sublanes():
    return lax.broadcasted_iota(jnp.int32, (8, 128), 0)


def prepare(pos, gate, resid_h, cell_h, azimuth_h, kxx_h, kyy_h, ksh_h, pay_a, pay_b, kt,
            resid, cell, azimuth, kxx, kyy, ksh, sems):
    copies = []

    def copy(src, dst):
        copies.append(pltpu.make_async_copy(src, dst, sems.at[len(copies)]))
        copies[-1].start()

    for src, dst in ((resid_h, resid), (cell_h, cell), (azimuth_h, azimuth)):
        copy(src, dst)
    tensors = ((kxx_h, kxx), (kyy_h, kyy), (ksh_h, ksh))
    size = 512 // PIECES
    for piece in range(PIECES):
        span = slice(piece * size, 520 if piece == PIECES - 1 else (piece + 1) * size)
        for src, dst in tensors:
            copy(src.at[span, :], dst.at[span, :])
    odd = (pos[0] & 1) == 1
    slot = lax.broadcasted_iota(jnp.int32, (32, 128), 0) * 128 + lax.broadcasted_iota(
        jnp.int32, (32, 128), 1
    )
    for ready in copies[:3]:
        ready.wait()
    weight = jnp.where(slot < gate[0, 0], resid[...], 0.0)
    angle = azimuth[...]
    wu = weight * jnp.sin(angle)
    wv = weight * jnp.cos(angle)
    cf = cell[...].astype(F32)
    for pay in (pay_a, pay_b):
        pay[0:32, :] = wu
        pay[32:64, :] = wv
        pay[64:96, :] = cf
        pay[TAIL + UNITS : PAY, :] = jnp.zeros((PAY - TAIL - UNITS, 128), F32)

    def entries(get):
        xx, yy = get(kxx), get(kyy)
        return xx, get(ksh) * jnp.sqrt(xx * yy), yy

    for piece in range(PIECES):
        for ready in copies[3 + 3 * piece : 6 + 3 * piece]:
            ready.wait()
        for tile in range(piece * NT // PIECES, (piece + 1) * NT // PIECES):
            rows = []
            for y in range(8):
                rows.append(entries(lambda ref: ref[pl.ds(tile * 64 + y, 8, stride=8), :]))
                for q in range(3):
                    start = (q * 8 + y) * 64 + tile * 8
                    kt[start : start + 8, :] = rows[y][q]
            for k in range(UNITS):
                start = 96 + k * 64 + tile * 8
                low, high = rows[LOW[k][0]][LOW[k][1]], rows[HIGH[k][0]][HIGH[k][1]]
                pay_a[start : start + 8, :] = jnp.where(odd, low, high)
                pay_b[start : start + 8, :] = jnp.where(odd, high, low)
    last = entries(lambda ref: ref[512:520, :])
    for q in range(3):
        kt[1536 + q * 8 : 1544 + q * 8, :] = last[q]
    for k in range(UNITS):
        start = TAIL + k
        low, high = (last[q][y : y + 1, :] for y, q in (LOW[k], HIGH[k]))
        pay_a[start : start + 1, :] = jnp.where(odd, low, high)
        pay_b[start : start + 1, :] = jnp.where(odd, high, low)


def scatter(jobs, tab, out_u, out_v):
    first = lax.broadcasted_iota(jnp.int32, (16, 128), 0).astype(F32)
    iota = [(first + 16.0 * b).astype(BF16) for b in range(8)]
    one = jnp.full((16, 128), 1, BF16)
    zero = jnp.full((16, 128), 0, BF16)
    per = KC // 128
    chunks = 4096 // KC
    for job, (wu, wv, cf, shift, ny, _) in enumerate(jobs):
        cell = cf.astype(jnp.int32)
        level = lax.shift_right_logical(cell, 10)
        row = (lax.shift_right_logical(cell, 7) & 7) - shift
        lf = level.astype(F32)
        index = [jnp.where((row == y) & (level < 64), lf, -1.0) for y in range(ny)]
        index += [jnp.full((32, 128), -1.0, F32)] * (8 - ny)
        index.append(jnp.where((level == 64) & (row < ny), row.astype(F32), -1.0))
        index.append((cell & 127).astype(F32))
        for value in (wu, wv):
            for _ in range(SPLITS):
                top = value.astype(BF16).astype(F32)
                value = value - top
                index.append(top)
        for k, value in enumerate(index):
            start = job * TAB + k * 32
            tab[start : start + 32, :] = value

    def build(job, c):
        ny = jobs[job][4]
        for j in range(per):

            def spread(k):
                i = job * TAB + k * 32 + c * per + j
                return jnp.broadcast_to(tab[i : i + 1, :], (16, 128)).astype(BF16)

            rows = []
            for y in range(ny):
                index = spread(y)
                for b in range(4):
                    rows.append(jnp.where(iota[b] == index, one, zero))
            rows.append(jnp.where(iota[0] == spread(8), one, zero))
            hot[job, c, j] = jnp.concatenate(rows, axis=0)
            col = spread(9)
            parts = [spread(10 + k) for k in range(2 * SPLITS)]
            hits = [iota[b] == col for b in range(8)]
            val[job, c, j] = jnp.concatenate(
                [
                    jnp.where(hit, parts[n * SPLITS + s], zero)
                    for s in range(SPLITS)
                    for n in range(2)
                    for hit in hits
                ],
                axis=0,
            )

    def multiply(job, c):
        ny, base = jobs[job][4:]
        count = ny * 64 + 16
        total = None
        left = jnp.concatenate([hot[job, c, j] for j in range(per)], axis=1)
        for s in range(SPLITS):
            part = lax.dot_general(
                left,
                jnp.concatenate(
                    [val[job, c, j][s * 256 : s * 256 + 256] for j in range(per)], axis=1
                ),
                (((1,), (1,)), ((), ())),
                preferred_element_type=F32,
            )
            total = part if total is None else total + part
        for ref, part in ((out_u, total[:, 0:128]), (out_v, total[:, 128:256])):
            if c > 0:
                part = part + ref[base : base + count, :]
            ref[base : base + count, :] = part

    hot, val = {}, {}
    steps = [(job, c) for job in range(len(jobs)) for c in range(chunks)]
    build(*steps[0])
    for now, later in zip(steps, steps[1:] + [None]):
        if later is not None:
            build(*later)
        multiply(*now)


def wind_at(own, halo, row, tile):
    if 0 <= row < 8:
        return wide(own, 512 + row) if tile is None else at(own, row * NT + tile)
    base, row = (0, row + 5) if row < 0 else (HALO, row - 8)
    if tile is None:
        return wide(halo, base + 320 + row)
    return at(halo, base // 8 + row * NT + tile)


def kappa_at(kt, halo, q, row, tile):
    if 0 <= row < 8:
        row = q * 8 + row
        return wide(kt, 1536 + row) if tile is None else at(kt, row * NT + tile)
    row = ((row + 4) if row < 0 else row - 4) * 3 + q
    return wide(halo, 1344 + row) if tile is None else at(halo, row * NT + tile)


def strip(get, ref, index):
    lane = lanes()
    left_slot = lane // 16
    right_slot = ((lane + 4) % 128) // 16
    left = right = None
    for j in range(8):
        moved = roll(get(j), 16 * j + 6)
        left = moved if j == 0 else jnp.where(left_slot == j, moved, left)
        right = moved if j == 0 else jnp.where(right_slot == j, moved, right)
    whole = get(None)
    last = jnp.where(sublanes() == 2, whole, roll(whole, 6))
    start = index * 24
    ref[start : start + 8, :] = left
    ref[start + 8 : start + 16, :] = right
    ref[start + 16 : start + 24, :] = last


def own_part(obs, kt, u, v, sw, sk, tab):
    job = (obs[0:32, :], obs[32:64, :], obs[64:96, :], 0, 8, 0)
    scatter([job], tab, u, v)
    for y in range(8):
        for n, ref in enumerate((u, v)):
            strip(lambda t: wind_at(ref, None, y, t), sw, n * 8 + y)
        for q in range(3):
            strip(lambda t: kappa_at(kt, None, q, y, t), sk, q * 8 + y)


def strip_place(k, sw, sk, tw, tk):
    if k < 36:
        n, row = k // 18, k % 18 - 5
        if 0 <= row < 8:
            return sw, n * 8 + row
        return tw, n * 10 + ((row + 5) if row < 0 else row - 3)
    q, row = (k - 36) // 15, (k - 36) % 15 - 4
    if 0 <= row < 8:
        return sk, q * 8 + row
    return tk, q * 7 + ((row + 4) if row < 0 else row - 4)


def message_rolls(t, width):
    place = width * t + (1 if width == 5 else 0)
    return place - (6 - width), place - 6


def near(pos, rec_a, u, v, tab):
    job = (rec_a[0:32, :], rec_a[32:64, :], rec_a[64:96, :], (pos[0] & 1) * 3, 5, 0)
    scatter([job], tab, u, v)


def edges(pos, rec_a, rec_b, au, av, sw, sk, hu, hv, kh, tw, tk, msg_c, msg_d, bu, bv, last, tab):
    odd = (pos[0] & 1) == 1
    for q in range(3):
        for j in range(7):
            dst, tail = (j * 3 + q) * 64, 1344 + j * 3 + q
            if j < 4 and (j + 4, q) not in HIGH:
                kh[dst : dst + 64, :] = jnp.zeros((64, 128), F32)
                kh[tail : tail + 1, :] = jnp.zeros((1, 128), F32)
                continue
            k = HIGH.index((j + 4, q)) if j < 4 else LOW.index((j - 4, q))
            one, two = (rec_a, rec_b) if j < 4 else (rec_b, rec_a)
            src = slice(96 + k * 64, 96 + k * 64 + 64)
            kh[dst : dst + 64, :] = jnp.where(odd, one[src, :], two[src, :])
            src = slice(TAIL + k, TAIL + k + 1)
            kh[tail : tail + 1, :] = jnp.where(odd, one[src, :], two[src, :])
    kh[1365:1368, :] = jnp.zeros((3, 128), F32)
    job = (rec_b[0:32, :], rec_b[32:64, :], rec_b[64:96, :], 3 - (pos[0] & 1) * 3, 5, 0)
    scatter([job], tab, bu, bv)
    for out, one, two in ((hu, au, bu), (hv, av, bv)):
        out[0:HALO, :] = jnp.where(odd, one[...], two[...])
        out[HALO : 2 * HALO, :] = jnp.where(odd, two[...], one[...])
    for i in range(10):
        row = i - 5 if i < 5 else i + 3
        for n, ref in enumerate((hu, hv)):
            strip(lambda t: wind_at(None, ref, row, t), tw, n * 10 + i)
    for i in range(7):
        row = i - 4 if i < 4 else i + 4
        for q in range(3):
            strip(lambda t: kappa_at(None, kh, q, row, t), tk, q * 7 + i)
    fifth = lanes() % 16
    odd_col = (pos[1] & 1) == 1
    for i, (members, width) in enumerate(GROUPS):
        packed = []
        for t, k in enumerate(members):
            ref, index = strip_place(k, sw, sk, tw, tk)
            left = ref[index * 24 : index * 24 + 8, :]
            packed.append([roll(left, by) for by in message_rolls(t, width)])
        right_edge, left_edge = packed[-1]
        for t in range(len(members) - 1, 0, -1):
            before = fifth < width * t + (1 if width == 5 else 0)
            right_edge = jnp.where(before, packed[t - 1][0], right_edge)
            left_edge = jnp.where(before, packed[t - 1][1], left_edge)
        msg_c[i * 8 : i * 8 + 8, :] = jnp.where(odd_col, left_edge, right_edge)
        msg_d[i * 8 : i * 8 + 8, :] = jnp.where(odd_col, right_edge, left_edge)
    for k in range(NQ):
        ref, index = strip_place(k, sw, sk, tw, tk)
        last[k : k + 1, :] = ref[index * 24 + 16 : index * 24 + 17, :]
    last[NQ : NQ + 7, :] = jnp.zeros((7, 128), F32)
    slot = lanes() // 16
    for g in range(2):
        packed = last[g * 64 : g * 64 + 8, :]
        for k in range(1, 8 if g == 0 else 3):
            start = g * 64 + k * 8
            packed = jnp.where(slot == k, roll(last[start : start + 8, :], 16 * k), packed)
        start = NM * 8 + g * 8
        msg_c[start : start + 8, :] = packed
        msg_d[start : start + 8, :] = packed


def derive(wind, low, high, mask, put):
    for row in range(-4, 12):
        side = low if row < 0 else high if row > 7 else None
        across = []
        along = []
        for n in range(2):
            here = wind(n, row)
            across.append(roll(here, -1) - roll(here, 1))
            along.append(wind(n, row + 1) - wind(n, row - 1))
        scale = 0.5 if side is None else 0.5 * side
        if mask is not None:
            scale = scale * mask
        put(0, row, scale * (along[0] - across[1]))
        put(1, row, -scale * (across[0] + along[1]))


def advance(more, field, kappa, high, mask, put):
    before = {}
    here = [field(n, -more - 1) for n in range(2)]
    for row in range(-more - 1, 8 + more):
        xx, xy, yy = (kappa(q, row) for q in range(3))
        for n in range(2):
            below = field(n, row + 1)
            gx = roll(here[n], -1) - here[n]
            gy = below - here[n]
            hx = xx * gx + xy * gy
            hy = xy * gx + yy * gy
            if row >= -more:
                value = here[n] - (roll(hx, 1) - hx + (before[n] - hy))
                if row > 7:
                    value = value * high
                if mask is not None:
                    value = value * mask
                put(n, row, value)
            before[n] = hy
            here[n] = below


def slab(ref, tiles, tile):
    def get(n, row):
        return at(ref, (n * 16 + row + 4) * tiles + tile)

    def put(n, row, value):
        start = ((n * 16 + row + 4) * tiles + tile) * 8
        ref[pl.ds(pl.multiple_of(start, 8), 8), :] = value

    return get, put


def ends(pos, size):
    low = jnp.where(pos[0] == 0, 0.0, 1.0).astype(F32)
    high = jnp.where(pos[0] == size - 1, 0.0, 1.0).astype(F32)
    return low, high


def middle(size, pos, u, v, hu, hv, kt, kh, main, fa, fb):
    low, high = ends(pos, size)
    wind_refs = ((u, hu), (v, hv))

    def stage(step):
        def body(g, _):
            for k in range(GROUP):
                tile = g * GROUP + k
                if step < 0:
                    put = slab(fa, NT, tile)[1]
                    derive(lambda n, row: wind_at(*wind_refs[n], row, tile), low, high, None, put)
                    continue
                src, dst = (fa, fb) if step % 2 == 0 else (fb, fa)
                put = slab(dst, NT, tile)[1]
                if step == STEPS - 1:

                    def put(n, row, value):
                        start = pl.multiple_of(((n * 8 + row) * NT + tile) * 8, 8)
                        main[pl.ds(start, 8), :] = value

                advance(
                    STEPS - 1 - step,
                    slab(src, NT, tile)[0],
                    lambda q, row: kappa_at(kt, kh, q, row, tile),
                    high,
                    None,
                    put,
                )
            return 0

        lax.fori_loop(0, NT // GROUP, body, 0)

    for step in range(-1, STEPS):
        stage(step)


def finish(
    rows, columns, pos, rec_c, rec_d, sw, sk, tw, tk, main, norm, result, mw, mk, masks, fa, fb, last_c, last_d, out, sems
):
    low, high = ends(pos, rows)
    odd_col = (pos[1] & 1) == 1
    lane = lanes()
    fifth = lane % 16
    sub = sublanes()
    take_left = (fifth >= 1) & (fifth <= 5)
    take_right = (fifth >= 6) & (fifth <= 10)
    take_last = (take_left & (sub == 0)) | (take_right & (sub == 1))
    for rec, unpacked in ((rec_c, last_c), (rec_d, last_d)):
        for k in range(11):
            start = NM * 8 + k // 8 * 8
            unpacked[k * 8 : k * 8 + 8, :] = roll(rec[start : start + 8, :], -16 * (k % 8))
    take = {}
    for width in (5, 4):
        take[width] = (
            (fifth >= 6 - width) & (fifth <= 5),
            (fifth >= 6) & (fifth <= 5 + width),
        )
    place = {}
    for i, (members, width) in enumerate(GROUPS):
        for t, k in enumerate(members):
            place[k] = i, t, width
    for k in range(NQ):
        src, index = strip_place(k, sw, sk, tw, tk)
        here = index * 24
        left, right = src[here : here + 8, :], src[here + 8 : here + 16, :]
        if k in place:
            i, t, width = place[k]
            a = rec_c[i * 8 : i * 8 + 8, :]
            b = rec_d[i * 8 : i * 8 + 8, :]
            right_by, left_by = message_rolls(t, width)
            left = jnp.where(take[width][0], roll(jnp.where(odd_col, a, b), -right_by), left)
            right = jnp.where(take[width][1], roll(jnp.where(odd_col, b, a), -left_by), right)
        last = jnp.where((sub == 0) == odd_col, wide(last_c, k), wide(last_d, k))
        dst, start = (mw, k * 24) if k < 36 else (mk, (k - 36) * 24)
        dst[start : start + 8, :] = left
        dst[start + 8 : start + 16, :] = right
        dst[start + 16 : start + 24, :] = jnp.where(take_last, last, src[here + 16 : here + 24, :])
    west = jnp.where(pos[1] == 0, 0.0, 1.0).astype(F32)
    east = jnp.where(pos[1] == columns - 1, 0.0, 1.0).astype(F32)
    left_mask = jnp.where(fifth < 6, west, 1.0)
    right_mask = jnp.where((fifth >= 6) & (fifth < 12), east, 1.0)
    masks[0:8, :] = left_mask
    masks[8:16, :] = right_mask
    masks[16:24, :] = jnp.where(sub == 0, left_mask, jnp.where(sub == 1, right_mask, 1.0))
    for step in range(-1, STEPS):
        for tile in range(3):
            mask = masks[tile * 8 : tile * 8 + 8, :]
            src, dst = (fa, fb) if step % 2 == 0 else (fb, fa)
            put = slab(dst, 3, tile)[1]
            if step < 0:
                derive(
                    lambda n, row: at(mw, (n * 18 + row + 5) * 3 + tile), low, high, mask, put
                )
            else:
                advance(
                    STEPS - 1 - step,
                    slab(src, 3, tile)[0],
                    lambda q, row: at(mk, (q * 15 + row + 4) * 3 + tile),
                    high,
                    mask,
                    put,
                )
    done = fb if STEPS % 2 == 1 else fa
    edge = (lane < 5) | (lane >= 123)
    copies = []
    for n in range(2):
        for y in range(8):
            left, right, last = (slab(done, 3, tile)[0](n, y) for tile in range(3))
            both = jnp.where(take_left, right, left)
            for tile in range(NT):
                place = ((n * 8 + y) * NT + tile) * 8
                value = jnp.where(edge, roll(both, -(16 * tile + 6)), main[place : place + 8, :])
                spot = pl.ds(n * 520 + tile * 64 + y, 8, stride=8)
                out[spot, :] = norm[spot, :] * value
            both = roll(jnp.where(take_left[0:1], last[1:2], last[0:1]), -6)
            value = jnp.where(edge[0:1], both, last[2:3])
            spot = n * 520 + 512 + y
            out[spot : spot + 1, :] = norm[spot : spot + 1, :] * value
        half = pl.ds(n * 520, 520)
        copies.append(pltpu.make_async_copy(out.at[half, :], result.at[half, :], sems.at[n]))
        copies[-1].start()
    for copy in copies:
        copy.wait()


def call(body, shapes, specs, scratch=(), cost=None, out_spec=VM):
    return pl.pallas_call(
        body,
        out_shape=[jax.ShapeDtypeStruct((n, 128), F32) for n in shapes],
        in_specs=specs,
        out_specs=[out_spec] * len(shapes),
        scratch_shapes=list(scratch),
        cost_estimate=cost,
        compiler_params=pltpu.CompilerParams(vmem_limit_bytes=32 << 20),
    )


def estimate(flops, bytes_accessed):
    return pl.CostEstimate(flops=flops, bytes_accessed=bytes_accessed, transcendentals=0)


def on_device(
    obs_resid, obs_cell, azimuth, gate_count, kappa_xx, kappa_yy, kappa_shear, norm_scale
):
    rows, columns = lax.axis_size("row"), lax.axis_size("col")
    pos = jnp.stack([lax.axis_index("row"), lax.axis_index("col")]).astype(jnp.int32)
    flat = lambda a: a.reshape(-1, 128)
    buffers = lambda *shapes: tuple(pltpu.VMEM((n, 128), t) for n, t in shapes)
    pay_a, pay_b, kt = call(
        prepare,
        (PAY, PAY, 24 * 64 + 24),
        [SM, SM] + [HB] * 6,
        buffers((32, F32), (32, jnp.int32), (32, F32), (520, F32), (520, F32), (520, F32))
        + (pltpu.SemaphoreType.DMA((3 + 3 * PIECES,)),),
    )(
        pos,
        gate_count,
        *(
            pltpu.with_memory_space_constraint(flat(a), pltpu.HBM)
            for a in (obs_resid, obs_cell, azimuth, kappa_xx, kappa_yy, kappa_shear)
        ),
    )
    rec_b = lax.ppermute(pay_b, "row", pairs(rows, 1))
    rec_a = lax.ppermute(pay_a, "row", pairs(rows, 0))
    work = buffers((TAB, F32))
    u, v, sw, sk = call(
        own_part,
        (OWN, OWN, 16 * 24, 24 * 24),
        [VM] * 2,
        work,
        estimate(3_000_000_000, 2_000_000),
    )(pay_a[0:96], kt)
    au, av = call(
        near, (HALO, HALO), [SM, VM], work, estimate(3_000_000_000, 2_000_000)
    )(pos, rec_a)
    hu, hv, kh, tw, tk, msg_c, msg_d = call(
        edges,
        (2 * HALO, 2 * HALO, 21 * 64 + 24, 20 * 24, 21 * 24, MSG, MSG),
        [SM] + [VM] * 6,
        buffers((HALO, F32), (HALO, F32), (88, F32)) + work,
    )(pos, rec_a, rec_b, au, av, sw, sk)
    rec_c = lax.ppermute(msg_c, "col", pairs(columns, 0))
    rec_d = lax.ppermute(msg_d, "col", pairs(columns, 1))
    (main,) = call(
        lambda *refs: middle(rows, *refs),
        (16 * 64,),
        [SM] + [VM] * 6,
        buffers((32 * 64, F32), (32 * 64, F32)),
        estimate(3_000_000_000, 4_000_000),
    )(pos, u, v, hu, hv, kt, kh)
    (out,) = call(
        lambda *refs: finish(rows, columns, *refs),
        (2 * 65 * 8,),
        [SM] + [VM] * 8,
        buffers((36 * 24, F32), (45 * 24, F32), (24, F32), (32 * 24, F32), (32 * 24, F32), (88, F32), (88, F32), (1040, F32))
        + (pltpu.SemaphoreType.DMA((2,)),),
        out_spec=HB,
    )(pos, rec_c, rec_d, sw, sk, tw, tk, main, flat(norm_scale))
    return out.reshape(norm_scale.shape)


def solution(mesh):
    in_specs = (
        P("row", "col"),
        P("row", "col"),
        P("row", "col"),
        P("row", "col"),
        P(None, "row", "col"),
        P(None, "row", "col"),
        P(None, "row", "col"),
        P(None, None, "row", "col"),
    )
    out_specs = P(None, None, "row", "col")
    return jax.shard_map(
        on_device, mesh=mesh, in_specs=in_specs, out_specs=out_specs, check_vma=False
    )
```

```python
import jax
import jax.numpy as jnp
from jax import lax
from jax.experimental import pallas as pl
from jax.experimental.pallas import tpu as pltpu
from jax.sharding import PartitionSpec as P


STEPS = 4
NT = 8
F32 = jnp.float32
BF16 = jnp.bfloat16
KC = 1024
SPLITS = 2
NQ = 81
GROUPS = [(list(range(k, k + 3)), 5) for k in range(0, 36, 3)]
GROUPS += [(list(range(k, k + 4)), 4) for k in range(37, NQ, 4)]
NM = len(GROUPS)
MSG = NM * 8 + 16
GROUP = 8
HIGH = [(row, q) for row in range(4, 8) for q in range(3)][1:]
LOW = [(row, q) for row in range(4) for q in range(3)][: len(HIGH)]
UNITS = len(HIGH)
TAIL = 96 + UNITS * 64
PAY = TAIL + 16
PIECES = 4
TAB = 320 + 64 * SPLITS
OWN = 8 * 64 + 16
HALO = 5 * 64 + 16
HB = pl.BlockSpec(memory_space=pltpu.HBM)
VM = pl.BlockSpec(memory_space=pltpu.VMEM)
SM = pl.BlockSpec(memory_space=pltpu.SMEM)


def pairs(size, first):
    out = []
    for i in range(first, size - 1, 2):
        out += [(i, i + 1), (i + 1, i)]
    return out


def roll(x, by):
    by = by % 128
    return x if by == 0 else pltpu.roll(x, by, 1)


def at(ref, i):
    return ref[pl.ds(pl.multiple_of(i * 8, 8), 8), :]


def wide(ref, row):
    return jnp.broadcast_to(ref[row : row + 1, :], (8, 128))


def lanes():
    return lax.broadcasted_iota(jnp.int32, (8, 128), 1)


def sublanes():
    return lax.broadcasted_iota(jnp.int32, (8, 128), 0)


def prepare(pos, gate, resid_h, cell_h, azimuth_h, kxx_h, kyy_h, ksh_h, pay_a, pay_b, kt,
            resid, cell, azimuth, kxx, kyy, ksh, sems):
    copies = []

    def copy(src, dst):
        copies.append(pltpu.make_async_copy(src, dst, sems.at[len(copies)]))
        copies[-1].start()

    for src, dst in ((resid_h, resid), (cell_h, cell), (azimuth_h, azimuth)):
        copy(src, dst)
    tensors = ((kxx_h, kxx), (kyy_h, kyy), (ksh_h, ksh))
    size = 512 // PIECES
    for piece in range(PIECES):
        span = slice(piece * size, 520 if piece == PIECES - 1 else (piece + 1) * size)
        for src, dst in tensors:
            copy(src.at[span, :], dst.at[span, :])
    odd = (pos[0] & 1) == 1
    slot = lax.broadcasted_iota(jnp.int32, (32, 128), 0) * 128 + lax.broadcasted_iota(
        jnp.int32, (32, 128), 1
    )
    for ready in copies[:3]:
        ready.wait()
    weight = jnp.where(slot < gate[0, 0], resid[...], 0.0)
    angle = azimuth[...]
    wu = weight * jnp.sin(angle)
    wv = weight * jnp.cos(angle)
    cf = cell[...].astype(F32)
    for pay in (pay_a, pay_b):
        pay[0:32, :] = wu
        pay[32:64, :] = wv
        pay[64:96, :] = cf
        pay[TAIL + UNITS : PAY, :] = jnp.zeros((PAY - TAIL - UNITS, 128), F32)

    def entries(get):
        xx, yy = get(kxx), get(kyy)
        return xx, get(ksh) * jnp.sqrt(xx * yy), yy

    for piece in range(PIECES):
        for ready in copies[3 + 3 * piece : 6 + 3 * piece]:
            ready.wait()
        for tile in range(piece * NT // PIECES, (piece + 1) * NT // PIECES):
            rows = []
            for y in range(8):
                rows.append(entries(lambda ref: ref[pl.ds(tile * 64 + y, 8, stride=8), :]))
                for q in range(3):
                    start = (q * 8 + y) * 64 + tile * 8
                    kt[start : start + 8, :] = rows[y][q]
            for k in range(UNITS):
                start = 96 + k * 64 + tile * 8
                low, high = rows[LOW[k][0]][LOW[k][1]], rows[HIGH[k][0]][HIGH[k][1]]
                pay_a[start : start + 8, :] = jnp.where(odd, low, high)
                pay_b[start : start + 8, :] = jnp.where(odd, high, low)
    last = entries(lambda ref: ref[512:520, :])
    for q in range(3):
        kt[1536 + q * 8 : 1544 + q * 8, :] = last[q]
    for k in range(UNITS):
        start = TAIL + k
        low, high = (last[q][y : y + 1, :] for y, q in (LOW[k], HIGH[k]))
        pay_a[start : start + 1, :] = jnp.where(odd, low, high)
        pay_b[start : start + 1, :] = jnp.where(odd, high, low)


def scatter(jobs, tab, out_u, out_v):
    first = lax.broadcasted_iota(jnp.int32, (16, 128), 0).astype(F32)
    iota = [(first + 16.0 * b).astype(BF16) for b in range(8)]
    one = jnp.full((16, 128), 1, BF16)
    zero = jnp.full((16, 128), 0, BF16)
    per = KC // 128
    chunks = 4096 // KC
    for job, (wu, wv, cf, shift, ny, _) in enumerate(jobs):
        cell = cf.astype(jnp.int32)
        level = lax.shift_right_logical(cell, 10)
        row = (lax.shift_right_logical(cell, 7) & 7) - shift
        lf = level.astype(F32)
        index = [jnp.where((row == y) & (level < 64), lf, -1.0) for y in range(ny)]
        index += [jnp.full((32, 128), -1.0, F32)] * (8 - ny)
        index.append(jnp.where((level == 64) & (row < ny), row.astype(F32), -1.0))
        index.append((cell & 127).astype(F32))
        for value in (wu, wv):
            for _ in range(SPLITS):
                top = value.astype(BF16).astype(F32)
                value = value - top
                index.append(top)
        for k, value in enumerate(index):
            start = job * TAB + k * 32
            tab[start : start + 32, :] = value

    def build(job, c):
        ny = jobs[job][4]
        for j in range(per):

            def spread(k):
                i = job * TAB + k * 32 + c * per + j
                return jnp.broadcast_to(tab[i : i + 1, :], (16, 128)).astype(BF16)

            rows = []
            for y in range(ny):
                index = spread(y)
                for b in range(4):
                    rows.append(jnp.where(iota[b] == index, one, zero))
            rows.append(jnp.where(iota[0] == spread(8), one, zero))
            hot[job, c, j] = jnp.concatenate(rows, axis=0)
            col = spread(9)
            parts = [spread(10 + k) for k in range(2 * SPLITS)]
            hits = [iota[b] == col for b in range(8)]
            val[job, c, j] = jnp.concatenate(
                [
                    jnp.where(hit, parts[n * SPLITS + s], zero)
                    for s in range(SPLITS)
                    for n in range(2)
                    for hit in hits
                ],
                axis=0,
            )

    def multiply(job, c):
        ny, base = jobs[job][4:]
        count = ny * 64 + 16
        total = None
        left = jnp.concatenate([hot[job, c, j] for j in range(per)], axis=1)
        for s in range(SPLITS):
            part = lax.dot_general(
                left,
                jnp.concatenate(
                    [val[job, c, j][s * 256 : s * 256 + 256] for j in range(per)], axis=1
                ),
                (((1,), (1,)), ((), ())),
                preferred_element_type=F32,
            )
            total = part if total is None else total + part
        for ref, part in ((out_u, total[:, 0:128]), (out_v, total[:, 128:256])):
            if c > 0:
                part = part + ref[base : base + count, :]
            ref[base : base + count, :] = part

    hot, val = {}, {}
    steps = [(job, c) for job in range(len(jobs)) for c in range(chunks)]
    build(*steps[0])
    for now, later in zip(steps, steps[1:] + [None]):
        if later is not None:
            build(*later)
        multiply(*now)


def wind_at(own, halo, row, tile):
    if 0 <= row < 8:
        return wide(own, 512 + row) if tile is None else at(own, row * NT + tile)
    base, row = (0, row + 5) if row < 0 else (HALO, row - 8)
    if tile is None:
        return wide(halo, base + 320 + row)
    return at(halo, base // 8 + row * NT + tile)


def kappa_at(kt, halo, q, row, tile):
    if 0 <= row < 8:
        row = q * 8 + row
        return wide(kt, 1536 + row) if tile is None else at(kt, row * NT + tile)
    row = ((row + 4) if row < 0 else row - 4) * 3 + q
    return wide(halo, 1344 + row) if tile is None else at(halo, row * NT + tile)


def strip(get, ref, index):
    lane = lanes()
    left_slot = lane // 16
    right_slot = ((lane + 4) % 128) // 16
    left = right = None
    for j in range(8):
        moved = roll(get(j), 16 * j + 6)
        left = moved if j == 0 else jnp.where(left_slot == j, moved, left)
        right = moved if j == 0 else jnp.where(right_slot == j, moved, right)
    whole = get(None)
    last = jnp.where(sublanes() == 2, whole, roll(whole, 6))
    start = index * 24
    ref[start : start + 8, :] = left
    ref[start + 8 : start + 16, :] = right
    ref[start + 16 : start + 24, :] = last


def own_part(obs, kt, u, v, sw, sk, tab):
    job = (obs[0:32, :], obs[32:64, :], obs[64:96, :], 0, 8, 0)
    scatter([job], tab, u, v)
    for y in range(8):
        for n, ref in enumerate((u, v)):
            strip(lambda t: wind_at(ref, None, y, t), sw, n * 8 + y)
        for q in range(3):
            strip(lambda t: kappa_at(kt, None, q, y, t), sk, q * 8 + y)


def strip_place(k, sw, sk, tw, tk):
    if k < 36:
        n, row = k // 18, k % 18 - 5
        if 0 <= row < 8:
            return sw, n * 8 + row
        return tw, n * 10 + ((row + 5) if row < 0 else row - 3)
    q, row = (k - 36) // 15, (k - 36) % 15 - 4
    if 0 <= row < 8:
        return sk, q * 8 + row
    return tk, q * 7 + ((row + 4) if row < 0 else row - 4)


def message_rolls(t, width):
    place = width * t + (1 if width == 5 else 0)
    return place - (6 - width), place - 6


def near(pos, rec_a, u, v, tab):
    job = (rec_a[0:32, :], rec_a[32:64, :], rec_a[64:96, :], (pos[0] & 1) * 3, 5, 0)
    scatter([job], tab, u, v)


def edges(pos, rec_a, rec_b, au, av, sw, sk, hu, hv, kh, tw, tk, msg_c, msg_d, bu, bv, last, tab):
    odd = (pos[0] & 1) == 1
    for q in range(3):
        for j in range(7):
            dst, tail = (j * 3 + q) * 64, 1344 + j * 3 + q
            if j < 4 and (j + 4, q) not in HIGH:
                kh[dst : dst + 64, :] = jnp.zeros((64, 128), F32)
                kh[tail : tail + 1, :] = jnp.zeros((1, 128), F32)
                continue
            k = HIGH.index((j + 4, q)) if j < 4 else LOW.index((j - 4, q))
            one, two = (rec_a, rec_b) if j < 4 else (rec_b, rec_a)
            src = slice(96 + k * 64, 96 + k * 64 + 64)
            kh[dst : dst + 64, :] = jnp.where(odd, one[src, :], two[src, :])
            src = slice(TAIL + k, TAIL + k + 1)
            kh[tail : tail + 1, :] = jnp.where(odd, one[src, :], two[src, :])
    kh[1365:1368, :] = jnp.zeros((3, 128), F32)
    job = (rec_b[0:32, :], rec_b[32:64, :], rec_b[64:96, :], 3 - (pos[0] & 1) * 3, 5, 0)
    scatter([job], tab, bu, bv)
    for out, one, two in ((hu, au, bu), (hv, av, bv)):
        out[0:HALO, :] = jnp.where(odd, one[...], two[...])
        out[HALO : 2 * HALO, :] = jnp.where(odd, two[...], one[...])
    for i in range(10):
        row = i - 5 if i < 5 else i + 3
        for n, ref in enumerate((hu, hv)):
            strip(lambda t: wind_at(None, ref, row, t), tw, n * 10 + i)
    for i in range(7):
        row = i - 4 if i < 4 else i + 4
        for q in range(3):
            strip(lambda t: kappa_at(None, kh, q, row, t), tk, q * 7 + i)
    fifth = lanes() % 16
    odd_col = (pos[1] & 1) == 1
    for i, (members, width) in enumerate(GROUPS):
        packed = []
        for t, k in enumerate(members):
            ref, index = strip_place(k, sw, sk, tw, tk)
            left = ref[index * 24 : index * 24 + 8, :]
            packed.append([roll(left, by) for by in message_rolls(t, width)])
        right_edge, left_edge = packed[-1]
        for t in range(len(members) - 1, 0, -1):
            before = fifth < width * t + (1 if width == 5 else 0)
            right_edge = jnp.where(before, packed[t - 1][0], right_edge)
            left_edge = jnp.where(before, packed[t - 1][1], left_edge)
        msg_c[i * 8 : i * 8 + 8, :] = jnp.where(odd_col, left_edge, right_edge)
        msg_d[i * 8 : i * 8 + 8, :] = jnp.where(odd_col, right_edge, left_edge)
    for k in range(NQ):
        ref, index = strip_place(k, sw, sk, tw, tk)
        last[k : k + 1, :] = ref[index * 24 + 16 : index * 24 + 17, :]
    last[NQ : NQ + 7, :] = jnp.zeros((7, 128), F32)
    slot = lanes() // 16
    for g in range(2):
        packed = last[g * 64 : g * 64 + 8, :]
        for k in range(1, 8 if g == 0 else 3):
            start = g * 64 + k * 8
            packed = jnp.where(slot == k, roll(last[start : start + 8, :], 16 * k), packed)
        start = NM * 8 + g * 8
        msg_c[start : start + 8, :] = packed
        msg_d[start : start + 8, :] = packed


def derive(wind, low, high, mask, put):
    for row in range(-4, 12):
        side = low if row < 0 else high if row > 7 else None
        across = []
        along = []
        for n in range(2):
            here = wind(n, row)
            across.append(roll(here, -1) - roll(here, 1))
            along.append(wind(n, row + 1) - wind(n, row - 1))
        scale = 0.5 if side is None else 0.5 * side
        if mask is not None:
            scale = scale * mask
        put(0, row, scale * (along[0] - across[1]))
        put(1, row, -scale * (across[0] + along[1]))


def advance(more, field, kappa, high, mask, put):
    before = {}
    here = [field(n, -more - 1) for n in range(2)]
    for row in range(-more - 1, 8 + more):
        xx, xy, yy = (kappa(q, row) for q in range(3))
        for n in range(2):
            below = field(n, row + 1)
            gx = roll(here[n], -1) - here[n]
            gy = below - here[n]
            hx = xx * gx + xy * gy
            hy = xy * gx + yy * gy
            if row >= -more:
                value = here[n] - (roll(hx, 1) - hx + (before[n] - hy))
                if row > 7:
                    value = value * high
                if mask is not None:
                    value = value * mask
                put(n, row, value)
            before[n] = hy
            here[n] = below


def slab(ref, tiles, tile):
    def get(n, row):
        return at(ref, (n * 16 + row + 4) * tiles + tile)

    def put(n, row, value):
        start = ((n * 16 + row + 4) * tiles + tile) * 8
        ref[pl.ds(pl.multiple_of(start, 8), 8), :] = value

    return get, put


def ends(pos, size):
    low = jnp.where(pos[0] == 0, 0.0, 1.0).astype(F32)
    high = jnp.where(pos[0] == size - 1, 0.0, 1.0).astype(F32)
    return low, high


def middle(size, pos, u, v, hu, hv, kt, kh, main, fa, fb):
    low, high = ends(pos, size)
    wind_refs = ((u, hu), (v, hv))

    def stage(step):
        def body(g, _):
            for k in range(GROUP):
                tile = g * GROUP + k
                if step < 0:
                    put = slab(fa, NT, tile)[1]
                    derive(lambda n, row: wind_at(*wind_refs[n], row, tile), low, high, None, put)
                    continue
                src, dst = (fa, fb) if step % 2 == 0 else (fb, fa)
                put = slab(dst, NT, tile)[1]
                if step == STEPS - 1:

                    def put(n, row, value):
                        start = pl.multiple_of(((n * 8 + row) * NT + tile) * 8, 8)
                        main[pl.ds(start, 8), :] = value

                advance(
                    STEPS - 1 - step,
                    slab(src, NT, tile)[0],
                    lambda q, row: kappa_at(kt, kh, q, row, tile),
                    high,
                    None,
                    put,
                )
            return 0

        lax.fori_loop(0, NT // GROUP, body, 0)

    for step in range(-1, STEPS):
        stage(step)


def fill_side(is_left, rec, sw, sk, tw, tk, mw, mk, tiles):
    fifth = lanes() % 16
    place = {}
    for i, (members, width) in enumerate(GROUPS):
        for t, k in enumerate(members):
            place[k] = i, t, width
    take = {}
    for width in (5, 4):
        start = jnp.where(is_left, 6 - width, 6)
        take[width] = (fifth >= start) & (fifth < start + width)
    for k in range(NQ):
        src, index = strip_place(k, sw, sk, tw, tk)
        here = index * 24
        own = jnp.where(is_left, src[here : here + 8, :], src[here + 8 : here + 16, :])
        if k in place:
            i, t, width = place[k]
            right_by, left_by = message_rolls(t, width)
            by = jnp.where(is_left, -right_by % 128, -left_by % 128)
            own = jnp.where(take[width], pltpu.roll(rec[i * 8 : i * 8 + 8, :], by, 1), own)
        dst, start = (mw, k * tiles * 8) if k < 36 else (mk, (k - 36) * tiles * 8)
        dst[start : start + 8, :] = own


def side_masks(pos, columns):
    fifth = lanes() % 16
    west = jnp.where(pos[1] == 0, 0.0, 1.0).astype(F32)
    east = jnp.where(pos[1] == columns - 1, 0.0, 1.0).astype(F32)
    return (
        jnp.where(fifth < 6, west, 1.0),
        jnp.where((fifth >= 6) & (fifth < 12), east, 1.0),
    )


def diffuse_strips(tiles, masks, mw, mk, fa, fb, low, high):
    for step in range(-1, STEPS):
        for tile in range(tiles):
            src, dst = (fa, fb) if step % 2 == 0 else (fb, fa)
            put = slab(dst, tiles, tile)[1]
            if step < 0:
                derive(
                    lambda n, row: at(mw, (n * 18 + row + 5) * tiles + tile),
                    low,
                    high,
                    masks[tile],
                    put,
                )
            else:
                advance(
                    STEPS - 1 - step,
                    slab(src, tiles, tile)[0],
                    lambda q, row: at(mk, (q * 15 + row + 4) * tiles + tile),
                    high,
                    masks[tile],
                    put,
                )


def first_side(rows, columns, pos, rec_c, sw, sk, tw, tk, fa, mw, mk, fb):
    low, high = ends(pos, rows)
    odd_col = (pos[1] & 1) == 1
    fill_side(odd_col, rec_c, sw, sk, tw, tk, mw, mk, 1)
    left_mask, right_mask = side_masks(pos, columns)
    diffuse_strips(1, [jnp.where(odd_col, left_mask, right_mask)], mw, mk, fa, fb, low, high)


def finish(
    rows, columns, pos, rec_c, rec_d, sw, sk, tw, tk, one, main, norm, result, mw, mk, fa, fb,
    last_c, last_d, out, sems
):
    low, high = ends(pos, rows)
    odd_col = (pos[1] & 1) == 1
    lane = lanes()
    fifth = lane % 16
    sub = sublanes()
    take_left = (fifth >= 1) & (fifth <= 5)
    take_right = (fifth >= 6) & (fifth <= 10)
    take_last = (take_left & (sub == 0)) | (take_right & (sub == 1))
    fill_side(jnp.logical_not(odd_col), rec_d, sw, sk, tw, tk, mw, mk, 2)
    for rec, unpacked in ((rec_c, last_c), (rec_d, last_d)):
        for k in range(11):
            start = NM * 8 + k // 8 * 8
            unpacked[k * 8 : k * 8 + 8, :] = roll(rec[start : start + 8, :], -16 * (k % 8))
    for k in range(NQ):
        src, index = strip_place(k, sw, sk, tw, tk)
        here = index * 24 + 16
        last = jnp.where((sub == 0) == odd_col, wide(last_c, k), wide(last_d, k))
        dst, start = (mw, k * 16 + 8) if k < 36 else (mk, (k - 36) * 16 + 8)
        dst[start : start + 8, :] = jnp.where(take_last, last, src[here : here + 8, :])
    left_mask, right_mask = side_masks(pos, columns)
    masks = [
        jnp.where(odd_col, right_mask, left_mask),
        jnp.where(sub == 0, left_mask, jnp.where(sub == 1, right_mask, 1.0)),
    ]
    diffuse_strips(2, masks, mw, mk, fa, fb, low, high)
    edge = (lane < 5) | (lane >= 123)
    copies = []
    for n in range(2):
        for y in range(8):
            near_side = slab(one, 1, 0)[0](n, y)
            other, last = (slab(fa, 2, tile)[0](n, y) for tile in range(2))
            both = jnp.where(take_left == odd_col, other, near_side)
            for tile in range(NT):
                place = ((n * 8 + y) * NT + tile) * 8
                value = jnp.where(edge, roll(both, -(16 * tile + 6)), main[place : place + 8, :])
                spot = pl.ds(n * 520 + tile * 64 + y, 8, stride=8)
                out[spot, :] = norm[spot, :] * value
            both = roll(jnp.where(take_left[0:1], last[1:2], last[0:1]), -6)
            value = jnp.where(edge[0:1], both, last[2:3])
            spot = n * 520 + 512 + y
            out[spot : spot + 1, :] = norm[spot : spot + 1, :] * value
        half = pl.ds(n * 520, 520)
        copies.append(pltpu.make_async_copy(out.at[half, :], result.at[half, :], sems.at[n]))
        copies[-1].start()
    for copy in copies:
        copy.wait()


def call(body, shapes, specs, scratch=(), cost=None, out_spec=VM):
    return pl.pallas_call(
        body,
        out_shape=[jax.ShapeDtypeStruct((n, 128), F32) for n in shapes],
        in_specs=specs,
        out_specs=[out_spec] * len(shapes),
        scratch_shapes=list(scratch),
        cost_estimate=cost,
        compiler_params=pltpu.CompilerParams(vmem_limit_bytes=32 << 20),
    )


def estimate(flops, bytes_accessed):
    return pl.CostEstimate(flops=flops, bytes_accessed=bytes_accessed, transcendentals=0)


def on_device(
    obs_resid, obs_cell, azimuth, gate_count, kappa_xx, kappa_yy, kappa_shear, norm_scale
):
    rows, columns = lax.axis_size("row"), lax.axis_size("col")
    pos = jnp.stack([lax.axis_index("row"), lax.axis_index("col")]).astype(jnp.int32)
    flat = lambda a: a.reshape(-1, 128)
    buffers = lambda *shapes: tuple(pltpu.VMEM((n, 128), t) for n, t in shapes)
    pay_a, pay_b, kt = call(
        prepare,
        (PAY, PAY, 24 * 64 + 24),
        [SM, SM] + [HB] * 6,
        buffers((32, F32), (32, jnp.int32), (32, F32), (520, F32), (520, F32), (520, F32))
        + (pltpu.SemaphoreType.DMA((3 + 3 * PIECES,)),),
    )(
        pos,
        gate_count,
        *(
            pltpu.with_memory_space_constraint(flat(a), pltpu.HBM)
            for a in (obs_resid, obs_cell, azimuth, kappa_xx, kappa_yy, kappa_shear)
        ),
    )
    rec_b = lax.ppermute(pay_b, "row", pairs(rows, 1))
    rec_a = lax.ppermute(pay_a, "row", pairs(rows, 0))
    work = buffers((TAB, F32))
    u, v, sw, sk = call(
        own_part,
        (OWN, OWN, 16 * 24, 24 * 24),
        [VM] * 2,
        work,
        estimate(3_000_000_000, 2_000_000),
    )(pay_a[0:96], kt)
    au, av = call(
        near, (HALO, HALO), [SM, VM], work, estimate(3_000_000_000, 2_000_000)
    )(pos, rec_a)
    hu, hv, kh, tw, tk, msg_c, msg_d = call(
        edges,
        (2 * HALO, 2 * HALO, 21 * 64 + 24, 20 * 24, 21 * 24, MSG, MSG),
        [SM] + [VM] * 6,
        buffers((HALO, F32), (HALO, F32), (88, F32)) + work,
    )(pos, rec_a, rec_b, au, av, sw, sk)
    rec_c = lax.ppermute(msg_c, "col", pairs(columns, 0))
    rec_d = lax.ppermute(msg_d, "col", pairs(columns, 1))
    (main,) = call(
        lambda *refs: middle(rows, *refs),
        (16 * 64,),
        [SM] + [VM] * 6,
        buffers((32 * 64, F32), (32 * 64, F32)),
        estimate(3_000_000_000, 4_000_000),
    )(pos, u, v, hu, hv, kt, kh)
    (one,) = call(
        lambda *refs: first_side(rows, columns, *refs),
        (32 * 8,),
        [SM] + [VM] * 5,
        buffers((36 * 8, F32), (45 * 8, F32), (32 * 8, F32)),
        estimate(2_000_000_000, 2_000_000),
    )(pos, rec_c, sw, sk, tw, tk)
    (out,) = call(
        lambda *refs: finish(rows, columns, *refs),
        (2 * 65 * 8,),
        [SM] + [VM] * 9,
        buffers((36 * 16, F32), (45 * 16, F32), (32 * 16, F32), (32 * 16, F32), (88, F32), (88, F32), (1040, F32))
        + (pltpu.SemaphoreType.DMA((2,)),),
        out_spec=HB,
    )(pos, rec_c, rec_d, sw, sk, tw, tk, one, main, flat(norm_scale))
    return out.reshape(norm_scale.shape)


def solution(mesh):
    in_specs = (
        P("row", "col"),
        P("row", "col"),
        P("row", "col"),
        P("row", "col"),
        P(None, "row", "col"),
        P(None, "row", "col"),
        P(None, "row", "col"),
        P(None, None, "row", "col"),
    )
    out_specs = P(None, None, "row", "col")
    return jax.shard_map(
        on_device, mesh=mesh, in_specs=in_specs, out_specs=out_specs, check_vma=False
    )
```
